256 devices in a mesh: elem: 16 (over y_lo, z), pts: 16 (over y_hi, x, core).
Axes of the slice: x: 4, y: 4 (y_hi: 2, y_lo: 2; y = y_hi * 2 + y_lo), z: 8, core: 2. Of those that a mesh axis runs over, the one named last changes fastest.
Arguments:
- basis: float32 [64, 8192, 256], P('elem', 'pts'), may hold values from -6 to 6
- applied: float32 [64, 8192, 256], P('elem', 'pts'), may hold values from -6 to 6
- quad: float32 [64, 8192], P('elem', 'pts'), may hold values from 0.00017263349 to 0.00069053395
- face_index: int32 [64, 4, 1024], P('elem', None, 'pts'), may hold values from 0 to 511
- face_pairing: int32 [64, 1024], P('elem', 'pts'), may hold values from 0 to 63, as said below
- orbitals: float32 [16384, 2048], P('elem', 'pts'), may hold values from -6 to 6
Outputs:
- filtered: float32 [16384, 2048], P('elem', 'pts')
The draws below stay inside these ranges and needn't reach their ends.
Inputs may be any that keep to these rules, and one draw needn't show every extreme that they name: `face_pairing`: each aligned block of 64 entries of a row is a permutation of 0 to 63.
All inputs are finite; a program needn't handle non-finite values.
Results may differ from the reference program's by a relative error of at most 0.0003.
Values sent between devices are 32-bit elements; how exact they have to be, the bound alone decides.
A program may use at most 64 MiB of HBM per device.

```python
import math
import jax
import jax.numpy as jnp
from jax import lax

NB = 256
NORB = 2048
DEG = 4
PTS_DEV = 512
FACE_DEV = 64
NELEM = 64
NPTS = 8192
FACES = 1024


def draw_face_pairing(key, part):
    blocks = FACES // FACE_DEV
    keys = jax.random.split(jax.random.fold_in(key, 7), NELEM * blocks)
    perms = jax.vmap(lambda single: jax.random.permutation(single, FACE_DEV))(keys)
    return perms.reshape(NELEM, FACES).astype(jnp.int32)


def set_ends(values, key, least, top_value):
    shape = values.shape
    index_at = [jax.random.randint(jax.random.fold_in(key, axis), (), 0, shape[axis]) for axis in range(len(shape))]
    values = values.at[tuple(index_at)].set(least)
    longest = shape.index(max(shape))
    index_at[longest] = (index_at[longest] + 1) % shape[longest]
    return values.at[tuple(index_at)].set(top_value)


def block_levels(own_key, shape, shards, least, largest):
    loudness, own = 1.0, jax.random.fold_in(own_key, 6)
    for axis_at, blocks in shards:
        draws = jnp.exp(jax.random.uniform(jax.random.fold_in(own, axis_at), (blocks,), jnp.float32, least / len(shards), largest / len(shards)))
        loudness = loudness * jnp.repeat(draws, shape[axis_at] // blocks).reshape([-1 if axis == axis_at else 1 for axis in range(len(shape))])
    return loudness


def gaussian(own_key, dims, width, reach, cuts=(), held_as=jnp.bfloat16):
    values = width * jax.random.normal(own_key, dims, jnp.float32)
    if cuts:
        values = values * block_levels(own_key, dims, cuts, -0.22, 0.18)
    return jnp.clip(values, -reach, reach).astype(held_as)


def setup_inputs(seed: int = 0) -> dict:
    arg_keys = jax.random.split(jax.random.key(seed), 7)
    basis = gaussian(arg_keys[0], (NELEM, NPTS, NB), 1.0, 6.0, ((0, 16), (1, 16)), jnp.float32)
    applied = gaussian(arg_keys[1], (NELEM, NPTS, NB), 1.0, 6.0, ((0, 16), (1, 16)), jnp.float32)
    quad = jnp.clip(jnp.exp(math.log(0.00069053395) - 1.3862944 * jax.random.uniform(arg_keys[2], (NELEM, NPTS), jnp.float32) ** block_levels(arg_keys[2], (NELEM, NPTS), ((0, 16), (1, 16)), -0.2, 0.2)), 0.00017263349, 0.00069053395)
    face_index = set_ends(jax.random.randint(arg_keys[3], (NELEM, 4, FACES), 0, PTS_DEV), jax.random.fold_in(arg_keys[3], 1), 0, PTS_DEV - 1).astype(jnp.int32)
    face_pairing = draw_face_pairing(jax.random.fold_in(arg_keys[6], 71), 0)
    orbitals = gaussian(arg_keys[5], (NELEM * NB, NORB), 1.0, 6.0, ((0, 16), (1, 16)), jnp.float32)
    return dict(basis=basis, applied=applied, quad=quad, face_index=face_index, face_pairing=face_pairing, orbitals=orbitals)


highest = lax.Precision.HIGHEST
penalty = 3.0
center = 4.0
half_width = 12.0


def inner(first, second):
    return jnp.dot(first.T, second, precision=highest)


def reference(basis, applied, quad, face_index, face_pairing, orbitals):
    shard_start = (jnp.arange(FACES) // FACE_DEV * PTS_DEV).astype(jnp.int32)
    pair_start = (jnp.arange(FACES) // FACE_DEV * FACE_DEV).astype(jnp.int32)
    faces_total = float(FACES)

    def element_blocks(index):
        following = (index + 1) % NELEM
        basis_own = basis[index]
        points = (face_index[index] + shard_start[None, :]).astype(jnp.int32)
        traces = basis_own[points]
        next_points = (face_index[following, 0:2] + shard_start[None, :]).astype(jnp.int32)
        next_traces = basis[following][next_points]
        order = (face_pairing[index] + pair_start).astype(jnp.int32)
        next_face = next_traces[0][order]
        next_deriv = (next_traces[0] - next_traces[1])[order]
        left_face = traces[0]
        left_deriv = traces[0] - traces[1]
        right_face = traces[2]
        right_deriv = traces[2] - traces[3]
        gram = jnp.dot((basis_own * quad[index][:, None]).T, applied[index], precision=highest)
        mixed = inner(left_deriv, left_face) + inner(right_deriv, right_face)
        own_block = penalty * (inner(left_face, left_face) + inner(right_face, right_face)) - 0.5 * (mixed + mixed.T)
        coupling = 0.5 * inner(right_deriv, next_face) - 0.5 * inner(right_face, next_deriv) - penalty * inner(right_face, next_face)
        return 0.5 * (gram + gram.T) + own_block / faces_total, coupling / faces_total

    volume, coupling = lax.map(element_blocks, jnp.arange(NELEM, dtype=jnp.int32))
    earlier = jnp.roll(coupling, 1, axis=0)

    def operate(field):
        above = jnp.roll(field, -1, axis=0)
        below = jnp.roll(field, 1, axis=0)
        result = jnp.einsum("eab,ebo->eao", volume, field, precision=highest)
        result = result + jnp.einsum("eab,ebo->eao", coupling, above, precision=highest)
        result = result + jnp.einsum("eba,ebo->eao", earlier, below, precision=highest)
        return (result - center * field) / half_width

    vector = orbitals.reshape(NELEM, NB, NORB)
    previous = vector
    current = operate(vector)
    for degree in range(1, DEG):
        upcoming = 2.0 * operate(current) - previous
        previous = current
        current = upcoming
    return current.reshape(NELEM * NB, NORB)
```

```python
import jax
import jax.numpy as jnp
from jax import lax
from jax.experimental import pallas as pl
from jax.experimental.pallas import tpu as pltpu
from jax.sharding import PartitionSpec as P

NB = 256
MESH = pl.DeviceIdType.MESH
F32 = jnp.float32
BF16 = jnp.bfloat16


def split(value):
    high = value.astype(BF16)
    low = (value - high.astype(F32)).astype(BF16)
    return high, low


def nn(left, right):
    return lax.dot_general(left, right, (((1,), (0,)), ((), ())), preferred_element_type=F32)


def nt(left, right):
    return lax.dot_general(left, right, (((1,), (1,)), ((), ())), preferred_element_type=F32)


def three(product, left, right):
    return product(left[0], right[0]) + (product(left[0], right[1]) + product(left[1], right[0]))


class Slots:
    def __init__(self):
        self.count = 0

    def take(self, number=1):
        first = self.count
        self.count += number
        return first


def layout():
    slots = Slots()
    table = {}
    for name, number in (
        ("lead", 1), ("vin", 1), ("vout", 1), ("pair", 2),
        ("relay", 4), ("raw", 4), ("final", 4), ("ysum", 2),
        ("gy0", 1), ("gxm0", 2), ("gxp0", 2), ("gf0", 2),
        ("gxm1", 2), ("gxp1", 2), ("gf1", 2), ("gy1", 4),
        ("up", 8), ("down", 8),
    ):
        table[name] = slots.take(number)
    return table, slots.count


TABLE, COPIES = layout()


def kernel(
    basis, applied, quad, face_index, face_pairing, orbitals, out,
    b_buf, a_buf, bq, tl, tr, part, pair_in, ring_in, y_in, blocks,
    vol, cpl, cplt, field, up_out, up_in, down_in,
    local, send, recv,
):
    elem = lax.axis_index("elem")
    pts = lax.axis_index("pts")
    core = lax.rem(pts, 2)
    x = lax.rem(pts // 2, 4)
    yh = pts // 8
    other = 1 - core

    def at(elem_to, yh_to, x_to, core_to):
        return {"elem": lax.rem(elem_to, 16), "pts": yh_to * 8 + lax.rem(x_to, 4) * 2 + core_to}

    partner = at(elem, yh, x, other)
    xm = at(elem, yh, x + 3, core)
    xp = at(elem, yh, x + 1, core)
    yp = at(elem, 1 - yh, x, core)
    after = at(elem + core, yh, x, other)
    before = at(elem + 15 + core, yh, x, other)
    far = at(elem + 15 + 2 * core, yh, x, other)
    em = at(elem + 15, yh, x, core)
    ep = at(elem + 1, yh, x, core)

    started = []

    def push(name, offset, source, target, device):
        index = TABLE[name] + offset
        copy = pltpu.make_async_remote_copy(
            src_ref=source, dst_ref=target, send_sem=send.at[index], recv_sem=recv.at[index],
            device_id=device, device_id_type=MESH,
        )
        copy.start()
        started.append(copy)

    def arrive(name, offset, target):
        index = TABLE[name] + offset
        pltpu.make_async_remote_copy(
            src_ref=target, dst_ref=target, send_sem=send.at[index], recv_sem=recv.at[index],
            device_id=partner, device_id_type=MESH,
        ).wait_recv()

    for e in range(4):
        pltpu.make_async_copy(basis.at[e], b_buf.at[e], local.at[e]).start()
    own_rows = pl.ds(pl.multiple_of(core * 512, 512), 512)
    other_rows = pl.ds(pl.multiple_of(other * 512, 512), 512)
    for i in range(4):
        e = lax.rem(i + 2 * other, 4)
        pltpu.make_async_copy(applied.at[e], a_buf.at[e], local.at[4 + e]).start()
    own_field = pltpu.make_async_copy(orbitals.at[own_rows], field.at[0, core], local.at[8])
    own_field.start()

    barrier = pltpu.get_barrier_semaphore()
    for device in (partner, xm, xp, yp, far, em, ep):
        pl.semaphore_signal(barrier, inc=1, device_id=device, device_id_type=MESH)

    point = lax.broadcasted_iota(jnp.int32, (512, NB), 0)
    lane = lax.broadcasted_iota(jnp.int32, (NB, 128), 1)

    def traces(e):
        pltpu.make_async_copy(basis.at[e], b_buf.at[e], local.at[e]).wait()
        turned = b_buf[e].T
        high, low = split(turned)
        picks = jnp.concatenate([face_index[e, r : r + 1, :] for r in range(4)], axis=1)
        chosen = jnp.where(point == picks, 1.0, 0.0).astype(BF16)
        values = nn(high, chosen) + nn(low, chosen)
        tl[e] = values[:, :128]
        tr[e] = values[:, 128:]
        high, low = split(turned * quad[pl.ds(e, 1), :])
        bq[0, e] = high
        bq[1, e] = low

    traces(0)
    pl.semaphore_wait(barrier, 7)
    push("lead", 0, tl.at[0], tl.at[4], em)
    push("vin", 0, orbitals.at[other_rows], field.at[0, core], partner)

    def traces_step(e, carry):
        traces(e)
        return carry

    lax.fori_loop(1, 4, traces_step, 0)

    def side(values):
        return jnp.where(lane < 64, 2.0 * values + pltpu.roll(values, 64, 1), 0.0) * (1.0 / 1024.0)

    def volume_at(half):
        def step(i, carry):
            e = lax.rem(i + 2 * half + 2 * other, 4)
            pltpu.make_async_copy(applied.at[e], a_buf.at[e], local.at[4 + e]).wait()
            total = three(nn, (bq[0, e], bq[1, e]), split(a_buf[e]))
            left, right = tl[e], tr[e]
            total = total + three(nt, split(side(left)), split(left))
            total = total + three(nt, split(side(right)), split(right))
            part[0, half, pl.ds(pl.multiple_of(i * NB, NB), NB), :] = total
            return carry

        lax.fori_loop(0, 2, step, 0)

    row = lax.broadcasted_iota(jnp.int32, (128, 128), 0)
    column = lax.broadcasted_iota(jnp.int32, (128, 128), 1)
    factor = jnp.where(
        row < 64, jnp.where(column < 64, -3.0, -0.5), jnp.where(column < 64, 0.5, 0.0)
    ) * (1.0 / 1024.0)
    slot = jnp.where(row < 64, row, row - 64)

    def coupling_at(half):
        def step(i, carry):
            e = lax.rem(i + 2 * half + 2 * other, 4)
            order = face_pairing[pl.ds(e, 1), :]
            order = jnp.concatenate([order, order], axis=1)
            mixing = jnp.where(slot == order, factor, 0.0).astype(BF16)
            high, low = split(tr[e])
            sides = nt(high, mixing) + nt(low, mixing)
            part[1, half, pl.ds(pl.multiple_of(i * NB, NB), NB), :] = three(nt, split(sides), split(tl[e + 1]))
            return carry

        lax.fori_loop(0, 2, step, 0)

    def rows(first, size):
        return pl.ds(pl.multiple_of(first, size), size)

    def near(t):
        return lax.rem(t, 4)

    sizes = (64, 32)

    def chunk(unit, t, s):
        if unit == 0:
            return rows((near(t) * 2 + s) * 64, 64)
        return rows(yh * 256 + near(t) * 64 + s * 32, 32)

    def short(unit):
        return pl.ds(0, sizes[unit])

    def ring_first(unit):
        acc = part.at[unit, 1]
        push("relay", unit * 2, acc.at[chunk(unit, x + 2, 0)], ring_in.at[unit, 0, short(unit)], xm)
        push("relay", unit * 2 + 1, acc.at[chunk(unit, x + 2, 1)], ring_in.at[unit, 1, short(unit)], xp)
        push("raw", unit * 2 + 1, acc.at[chunk(unit, x + 3, 1)], ring_in.at[unit, 3, short(unit)], xm)
        push("raw", unit * 2, acc.at[chunk(unit, x + 1, 0)], ring_in.at[unit, 2, short(unit)], xp)

    def ring_second(unit):
        n = sizes[unit]
        for s, shift, device in ((0, 3, xm), (1, 1, xp)):
            arrive("relay", unit * 2 + s, ring_in.at[unit, s, short(unit)])
            ring_in[unit, s, :n] = ring_in[unit, s, :n] + part[unit, 1, chunk(unit, x + shift, s), :]
            push("final", unit * 2 + s, ring_in.at[unit, s, short(unit)], ring_in.at[unit, 4 + s, short(unit)], device)

    def ring_last(unit):
        n = sizes[unit]
        for s in range(2):
            arrive("raw", unit * 2 + s, ring_in.at[unit, 2 + s, short(unit)])
            arrive("final", unit * 2 + s, ring_in.at[unit, 4 + s, short(unit)])
        for s in range(2):
            where = chunk(unit, x, s)
            part[unit, 1, where, :] = part[unit, 1, where, :] + ring_in[unit, 2 + s, :n] + ring_in[unit, 4 + s, :n]

    volume_at(0)
    push("pair", 0, part.at[0, 0], pair_in.at[0], partner)
    volume_at(1)
    arrive("pair", 0, pair_in.at[0])
    part[0, 1] = part[0, 1] + pair_in[0]
    ring_first(0)

    arrive("lead", 0, tl.at[4])
    coupling_at(0)
    push("pair", 1, part.at[1, 0], pair_in.at[1], partner)
    coupling_at(1)
    arrive("pair", 1, pair_in.at[1])
    part[1, 1] = part[1, 1] + pair_in[1]
    mine = rows(yh * 256, 256)
    theirs = rows((1 - yh) * 256, 256)
    push("ysum", 1, part.at[1, 1, theirs], y_in.at[1], yp)

    ring_second(0)

    arrive("ysum", 1, y_in.at[1])
    part[1, 1, mine, :] = part[1, 1, mine, :] + y_in[1]
    ring_first(1)

    ring_last(0)
    push("ysum", 0, part.at[0, 1, chunk(0, x, 1 - yh)], y_in.at[0, pl.ds(0, 64)], yp)

    ring_second(1)

    arrive("ysum", 0, y_in.at[0, pl.ds(0, 64)])
    here = chunk(0, x, yh)
    blocks[0, here, :] = part[0, 1, here, :] + y_in[0, :64]
    push("gy0", 0, blocks.at[0, here], blocks.at[0, here], yp)
    push("gxp0", yh, blocks.at[0, here], blocks.at[0, here], xm)
    push("gxm0", yh, blocks.at[0, here], blocks.at[0, here], xp)

    ring_last(1)
    strip = rows(yh * 256 + x * 64, 64)
    blocks[1, strip, :] = part[1, 1, strip, :]
    for s in range(2):
        piece = chunk(1, x, s)
        push("gxp1", s, blocks.at[1, piece], blocks.at[1, piece], xm)
        push("gxm1", s, blocks.at[1, piece], blocks.at[1, piece], xp)
    push("gy1", 0, blocks.at[1, strip], blocks.at[1, strip], yp)

    there = chunk(0, x, 1 - yh)
    arrive("gy0", 0, blocks.at[0, there])
    push("gxp0", 1 - yh, blocks.at[0, there], blocks.at[0, there], xm)
    push("gxm0", 1 - yh, blocks.at[0, there], blocks.at[0, there], xp)

    piece = chunk(1, x + 1, 0)
    arrive("gxp1", 0, blocks.at[1, piece])
    push("gf1", 0, blocks.at[1, piece], blocks.at[1, piece], xm)
    piece = chunk(1, x + 3, 1)
    arrive("gxm1", 1, blocks.at[1, piece])
    push("gf1", 1, blocks.at[1, piece], blocks.at[1, piece], xp)
    arrive("gxp1", 1, blocks.at[1, chunk(1, x + 1, 1)])
    arrive("gxm1", 0, blocks.at[1, chunk(1, x + 3, 0)])
    for number, shift in ((1, 1), (2, 3)):
        strip = rows(yh * 256 + near(x + shift) * 64, 64)
        push("gy1", number, blocks.at[1, strip], blocks.at[1, strip], yp)
    piece = chunk(0, x + 1, 0)
    arrive("gxp0", 0, blocks.at[0, piece])
    push("gf0", 0, blocks.at[0, piece], blocks.at[0, piece], xm)
    piece = chunk(0, x + 3, 1)
    arrive("gxm0", 1, blocks.at[0, piece])
    push("gf0", 1, blocks.at[0, piece], blocks.at[0, piece], xp)
    for s in range(2):
        arrive("gf1", s, blocks.at[1, chunk(1, x + 2, s)])
    strip = rows(yh * 256 + near(x + 2) * 64, 64)
    push("gy1", 3, blocks.at[1, strip], blocks.at[1, strip], yp)
    arrive("gxp0", 1, blocks.at[0, chunk(0, x + 1, 1)])
    arrive("gxm0", 0, blocks.at[0, chunk(0, x + 3, 0)])
    for s in range(2):
        arrive("gf0", s, blocks.at[0, chunk(0, x + 2, s)])

    diagonal = jnp.where(
        lax.broadcasted_iota(jnp.int32, (NB, NB), 0) == lax.broadcasted_iota(jnp.int32, (NB, NB), 1), 4.0 / 12.0, 0.0
    )
    for k in range(2):
        gram = blocks[0, k * NB : (k + 1) * NB, :]
        high, low = split((gram + gram.T) * (0.5 / 12.0) - diagonal)
        vol[0, k] = high
        vol[1, k] = low

    for number, shift in ((0, 0), (1, 1), (2, 3), (3, 2)):
        strip = rows((1 - yh) * 256 + near(x + shift) * 64, 64)
        arrive("gy1", number, blocks.at[1, strip])
    for k in range(2):
        block = blocks[1, k * NB : (k + 1) * NB, :] * (1.0 / 12.0)
        high, low = split(block)
        cpl[0, k] = high
        cpl[1, k] = low
        high, low = split(block.T)
        cplt[0, k] = high
        cplt[1, k] = low

    own_field.wait()
    arrive("vin", 0, field.at[0, other])

    def doubled(value):
        high, low = split(value)
        return jnp.concatenate([high, low], axis=1)

    def times(matrix, k, pair):
        both = nn(matrix[0, k], pair)
        return both[:, :128] + (both[:, 128:] + nn(matrix[1, k], pair[:, :128]))

    def offer(n, j):
        up_out[n, j] = times(cplt, 1, doubled(field[n, j, rows(256, 256), :]))
        index = n * 2 + j
        pltpu.make_async_remote_copy(
            src_ref=up_out.at[n, j], dst_ref=up_in.at[n, j], send_sem=send.at[TABLE["up"] + index],
            recv_sem=recv.at[TABLE["up"] + index], device_id=after, device_id_type=MESH,
        ).start()
        pltpu.make_async_remote_copy(
            src_ref=field.at[n, j, pl.ds(0, 256)], dst_ref=down_in.at[n, j], send_sem=send.at[TABLE["down"] + index],
            recv_sem=recv.at[TABLE["down"] + index], device_id=before, device_id_type=MESH,
        ).start()

    def advance(n, j):
        lower = doubled(field[n, j, rows(0, 256), :])
        upper = doubled(field[n, j, rows(256, 256), :])
        first = times(vol, 0, lower) + times(cpl, 0, upper)
        second = times(vol, 1, upper) + times(cplt, 0, lower)
        index = n * 2 + j
        arrive("up", index, up_in.at[n, j])
        arrive("down", index, down_in.at[n, j])
        first = first + up_in[n, j]
        second = second + times(cpl, 1, doubled(down_in[n, j]))
        return first, second

    def store(n, j, first, second):
        field[n, j, rows(0, 256), :] = first
        field[n, j, rows(256, 256), :] = second

    for j in range(2):
        offer(0, j)
    for j in range(2):
        first, second = advance(0, j)
        store(1, j, first, second)
        offer(1, j)

    def later(n, j):
        first, second = advance(n, j)
        first = 2.0 * first - field[n - 1, j, rows(0, 256), :]
        second = 2.0 * second - field[n - 1, j, rows(256, 256), :]
        store(n + 1, j, first, second)

    def round_trip(n, carry):
        for j in range(2):
            later(n, j)
            offer(n + 1, j)
        return carry

    lax.fori_loop(1, 3, round_trip, 0)
    for j in range(2):
        later(3, j)

    push("vout", 0, field.at[4, other], out.at[own_rows], partner)
    result = pltpu.make_async_copy(field.at[4, core], out.at[own_rows], local.at[9])
    result.start()
    for n in range(4):
        for j in range(2):
            index = n * 2 + j
            pltpu.make_async_remote_copy(
                src_ref=up_out.at[n, j], dst_ref=up_in.at[n, j], send_sem=send.at[TABLE["up"] + index],
                recv_sem=recv.at[TABLE["up"] + index], device_id=after, device_id_type=MESH,
            ).wait_send()
            pltpu.make_async_remote_copy(
                src_ref=field.at[n, j, pl.ds(0, 256)], dst_ref=down_in.at[n, j], send_sem=send.at[TABLE["down"] + index],
                recv_sem=recv.at[TABLE["down"] + index], device_id=before, device_id_type=MESH,
            ).wait_send()
    for copy in started:
        copy.wait_send()
    arrive("vout", 0, out.at[other_rows])
    result.wait()


def body(basis, applied, quad, face_index, face_pairing, orbitals):
    anywhere = pl.BlockSpec(memory_space=pl.ANY)
    held = pl.BlockSpec(memory_space=pltpu.VMEM)
    return pl.pallas_call(
        kernel,
        out_shape=jax.ShapeDtypeStruct(orbitals.shape, F32),
        in_specs=[anywhere, anywhere, held, held, held, anywhere],
        out_specs=anywhere,
        scratch_shapes=[
            pltpu.VMEM((4, 512, NB), F32),
            pltpu.VMEM((4, 512, NB), F32),
            pltpu.VMEM((2, 4, NB, 512), BF16),
            pltpu.VMEM((5, NB, 128), F32),
            pltpu.VMEM((4, NB, 128), F32),
            pltpu.VMEM((2, 2, 512, NB), F32),
            pltpu.VMEM((2, 512, NB), F32),
            pltpu.VMEM((2, 6, 64, NB), F32),
            pltpu.VMEM((2, 256, NB), F32),
            pltpu.VMEM((2, 512, NB), F32),
            pltpu.VMEM((2, 2, NB, NB), BF16),
            pltpu.VMEM((2, 2, NB, NB), BF16),
            pltpu.VMEM((2, 2, NB, NB), BF16),
            pltpu.VMEM((5, 2, 512, 128), F32),
            pltpu.VMEM((4, 2, NB, 128), F32),
            pltpu.VMEM((4, 2, NB, 128), F32),
            pltpu.VMEM((4, 2, NB, 128), F32),
            pltpu.SemaphoreType.DMA((10,)),
            pltpu.SemaphoreType.DMA((COPIES,)),
            pltpu.SemaphoreType.DMA((COPIES,)),
        ],
        name="filtered",
        compiler_params=pltpu.CompilerParams(collective_id=0, has_side_effects=True),
    )(basis, applied, quad, face_index, face_pairing, orbitals)


def solution(mesh):
    return jax.shard_map(
        body,
        mesh=mesh,
        in_specs=(
            P("elem", "pts", None),
            P("elem", "pts", None),
            P("elem", "pts"),
            P("elem", None, "pts"),
            P("elem", "pts"),
            P("elem", "pts"),
        ),
        out_specs=P("elem", "pts"),
        check_vma=False,
    )
```

```python
import jax
import jax.numpy as jnp
from jax import lax
from jax.experimental import pallas as pl
from jax.experimental.pallas import tpu as pltpu
from jax.sharding import PartitionSpec as P

NB = 256
MESH = pl.DeviceIdType.MESH
F32 = jnp.float32
BF16 = jnp.bfloat16


def split(value):
    high = value.astype(BF16)
    low = (value - high.astype(F32)).astype(BF16)
    return high, low


def nn(left, right):
    return lax.dot_general(left, right, (((1,), (0,)), ((), ())), preferred_element_type=F32)


def nt(left, right):
    return lax.dot_general(left, right, (((1,), (1,)), ((), ())), preferred_element_type=F32)


def three(product, left, right):
    return product(left[0], right[0]) + (product(left[0], right[1]) + product(left[1], right[0]))


class Slots:
    def __init__(self):
        self.count = 0

    def take(self, number=1):
        first = self.count
        self.count += number
        return first


def layout():
    slots = Slots()
    table = {}
    for name, number in (
        ("lead", 1), ("vin", 1), ("vout", 1), ("pair", 3),
        ("relay", 6), ("raw", 6), ("final", 6), ("ysum", 3),
        ("gy", 2), ("gx", 8), ("gf", 4),
        ("vx", 4), ("vf", 2), ("vy", 4),
        ("up", 8), ("down", 8),
    ):
        table[name] = slots.take(number)
    return table, slots.count


TABLE, COPIES = layout()


def kernel(
    basis, applied, quad_in, index_in, pairing_in, orbitals, out,
    b_buf, a_buf, quad, face_index, face_pairing, bq, ta, tb, tl, vpart, cpart, vpair, cpair, vring, cring, y_in, yc_in, vblock, cblock,
    near_part, up_part, down_part, field, near_sum, up_out, up_in, down_in,
    local, send, recv,
):
    elem = lax.axis_index("elem")
    pts = lax.axis_index("pts")
    core = lax.rem(pts, 2)
    x = lax.rem(pts // 2, 4)
    yh = pts // 8
    other = 1 - core

    def at(elem_to, yh_to, x_to, core_to):
        return {"elem": lax.rem(elem_to, 16), "pts": yh_to * 8 + lax.rem(x_to, 4) * 2 + core_to}

    partner = at(elem, yh, x, other)
    xm = at(elem, yh, x + 3, core)
    xp = at(elem, yh, x + 1, core)
    yp = at(elem, 1 - yh, x, core)
    after = at(elem + core, yh, x, other)
    before = at(elem + 15 + core, yh, x, other)
    far = at(elem + 15 + 2 * core, yh, x, other)
    em = at(elem + 15, yh, x, core)
    ep = at(elem + 1, yh, x, core)

    started = []

    def remote(name, offset, source, target, device):
        index = TABLE[name] + offset
        return pltpu.make_async_remote_copy(
            src_ref=source, dst_ref=target, send_sem=send.at[index], recv_sem=recv.at[index],
            device_id=device, device_id_type=MESH,
        )

    def push(name, offset, source, target, device):
        copy = remote(name, offset, source, target, device)
        copy.start()
        started.append(copy)

    def arrive(name, offset, target):
        remote(name, offset, target, target, partner).wait_recv()

    def sent(name, offset, source):
        remote(name, offset, source, source, partner).wait_send()

    small = [
        pltpu.make_async_copy(index_in, face_index, local.at[9]),
        pltpu.make_async_copy(quad_in, quad, local.at[10]),
        pltpu.make_async_copy(pairing_in, face_pairing, local.at[11]),
    ]
    for copy in small:
        copy.start()
    for e in range(4):
        pltpu.make_async_copy(basis.at[e], b_buf.at[e], local.at[e]).start()
    own_rows = pl.ds(pl.multiple_of(core * 512, 512), 512)
    other_rows = pl.ds(pl.multiple_of(other * 512, 512), 512)
    for i in range(4):
        e = lax.rem(i + 2 * other, 4)
        pltpu.make_async_copy(applied.at[e], a_buf.at[e], local.at[4 + e]).start()
    own_field = pltpu.make_async_copy(orbitals.at[own_rows], field.at[0, core], local.at[8])
    own_field.start()

    barrier = pltpu.get_barrier_semaphore()
    for device in (partner, xm, xp, yp, far, em, ep):
        pl.semaphore_signal(barrier, inc=1, device_id=device, device_id_type=MESH)

    point = lax.broadcasted_iota(jnp.int32, (512, NB), 0)
    lane = lax.broadcasted_iota(jnp.int32, (NB, 128), 1)

    def traces(e, carry):
        pltpu.make_async_copy(basis.at[e], b_buf.at[e], local.at[e]).wait()

        @pl.when(e == 0)
        def _():
            for copy in small:
                copy.wait()

        turned = b_buf[e].T
        high, low = split(turned)
        picks = jnp.concatenate([face_index[e, r : r + 1, :] for r in (0, 2, 1, 3)], axis=1)
        chosen = jnp.where(point == picks, 1.0, 0.0).astype(BF16)
        values = nn(high, chosen) + nn(low, chosen)
        faces, inside = values[:, :128], values[:, 128:]
        ta[e] = faces
        tb[e] = inside
        tl[e] = jnp.where(lane < 64, faces, pltpu.roll(inside, 64, 1))
        high, low = split(turned * quad[pl.ds(e, 1), :])
        bq[0, e] = high
        bq[1, e] = low
        return carry

    def rows(first, size):
        return pl.ds(pl.multiple_of(first, 8), size)

    def volumes(i, carry):
        e = lax.rem(i + 2 * other, 4)
        half = i // 2
        first = lax.rem(i, 2) * 192
        pltpu.make_async_copy(applied.at[e], a_buf.at[e], local.at[4 + e]).wait()
        faces = ta[e]
        total = three(nn, (bq[0, e], bq[1, e]), split(a_buf[e]))
        total = total + three(nt, split((2.0 * faces + tb[e]) * (1.0 / 1024.0)), split(faces))
        vpart[half, rows(first, 128), :128] = total[:128, :128]
        vpart[half, rows(first, 128), 128:] = total[:128, 128:] + total[128:, :128].T
        vpart[half, rows(first + 128, 64), :128] = total[128:192, 128:]
        vpart[half, rows(first + 128, 64), 128:] = total[192:, 128:]

        @pl.when((i == 1) & (depth > 0))
        def _():
            remote("pair", 0, vpart.at[0], vpair, partner).start()

        return carry

    row = lax.broadcasted_iota(jnp.int32, (128, NB), 0)
    column = lax.broadcasted_iota(jnp.int32, (128, NB), 1)
    factor = jnp.where(
        column < 128,
        jnp.where(column < 64, 0.0, jnp.where(row < 64, -3.0, 0.5)),
        jnp.where(column < 192, 0.0, jnp.where(row < 64, -0.5, 0.0)),
    ) * (1.0 / 1024.0)
    slot = jnp.where(row < 64, row, row - 64)

    def couplings(i, carry):
        e = jnp.where((core == 1) | (i == 3), i, lax.rem(i + 2, 3))
        half = jnp.where(e // 2 == core, 1, 0)
        k = lax.rem(e, 2)

        @pl.when(i == 3)
        def _():
            arrive("lead", 0, tl.at[4])

        order = face_pairing[pl.ds(e, 1), :]
        order = jnp.concatenate([order] * 4, axis=1)
        mixing = jnp.where(slot == order, factor, 0.0).astype(BF16)
        high, low = split(jnp.concatenate([ta[e], tb[e]], axis=1))
        sides = nt(high, mixing) + nt(low, mixing)
        mine = rows(k * NB, NB)
        cpart[half, mine, :] = three(nt, split(sides), split(tl[e + 1]))

        @pl.when(half == 0)
        def _():
            remote("pair", 1 + k, cpart.at[0, mine], cpair.at[mine], partner).start()

        return carry

    def near(t):
        return lax.rem(t, 4)

    sizes = (32, 32, 24)

    def chunk(unit, t, s):
        if unit == 2:
            return rows(yh * 192 + near(t) * 48 + s * 24, 24)
        return rows(unit * NB + (near(t) * 2 + s) * 32, 32)

    def strip(t, half):
        return rows(half * 192 + near(t) * 48, 48)

    def part(unit):
        return vpart.at[1] if unit == 2 else cpart.at[1]

    def ring(unit, k):
        return vring.at[k] if unit == 2 else cring.at[unit, k]

    def ring_first(unit):
        acc = part(unit)
        push("relay", unit * 2, acc.at[chunk(unit, x + 2, 0)], ring(unit, 0), xm)
        push("relay", unit * 2 + 1, acc.at[chunk(unit, x + 2, 1)], ring(unit, 1), xp)
        push("raw", unit * 2 + 1, acc.at[chunk(unit, x + 3, 1)], ring(unit, 3), xm)
        push("raw", unit * 2, acc.at[chunk(unit, x + 1, 0)], ring(unit, 2), xp)

    def ring_second(unit):
        for s, shift, device in ((0, 3, xm), (1, 1, xp)):
            passing = ring(unit, s)
            arrive("relay", unit * 2 + s, passing)
            passing[...] = passing[...] + part(unit)[chunk(unit, x + shift, s), :]
            push("final", unit * 2 + s, passing, ring(unit, 4 + s), device)

    def ring_last(unit, target):
        for s in range(2):
            arrive("raw", unit * 2 + s, ring(unit, 2 + s))
            arrive("final", unit * 2 + s, ring(unit, 4 + s))
            where = chunk(unit, x, s)
            target[where, :] = part(unit)[where, :] + ring(unit, 2 + s)[...] + ring(unit, 4 + s)[...]

    def share(name, offset, block, where, device):
        push(name, offset, block.at[where], block.at[where], device)

    def couple_first(unit):
        where = rows(unit * NB, NB)
        arrive("pair", 1 + unit, cpair.at[where])
        cpart[1, where, :] = cpart[1, where, :] + cpair[where, :]
        ring_first(unit)

    def couple_third(unit):
        ring_last(unit, cpart.at[1])
        push("ysum", unit, cpart.at[1, chunk(unit, x, 1 - yh)], yc_in.at[unit], yp)

    def couple_fourth(unit):
        arrive("ysum", unit, yc_in.at[unit])
        where = chunk(unit, x, yh)
        cblock[where, :] = cpart[1, where, :] + yc_in[unit]
        share("gy", unit, cblock, where, yp)
        share("gx", unit * 4 + yh, cblock, where, xm)
        share("gx", unit * 4 + 2 + yh, cblock, where, xp)

    def couple_fifth(unit):
        where = chunk(unit, x, 1 - yh)
        arrive("gy", unit, cblock.at[where])
        share("gx", unit * 4 + 1 - yh, cblock, where, xm)
        share("gx", unit * 4 + 3 - yh, cblock, where, xp)

    def couple_forward(unit, s):
        where = chunk(unit, x + 1 + 2 * s, s)
        arrive("gx", unit * 4 + 3 * s, cblock.at[where])
        share("gf", unit * 2 + s, cblock, where, at(elem, yh, x + 3 - 2 * s, core))

    def couple_end(unit):
        arrive("gx", unit * 4 + 1, cblock.at[chunk(unit, x + 1, 1)])
        arrive("gx", unit * 4 + 2, cblock.at[chunk(unit, x + 3, 0)])
        for s in range(2):
            arrive("gf", unit * 2 + s, cblock.at[chunk(unit, x + 2, s)])

    def meet():
        pl.semaphore_wait(barrier, 7)
        remote("lead", 0, tl.at[0], tl.at[4], em).start()

    depth = lax.rem(elem, 8)
    lax.fori_loop(0, 4, traces, 0)
    pl.when(depth > 0)(meet)
    lax.fori_loop(0, 4, volumes, 0)
    @pl.when(depth == 0)
    def _():
        meet()
        remote("pair", 0, vpart.at[0], vpair, partner).start()

    arrive("pair", 0, vpair)
    vpart[1] = vpart[1] + vpair[...]
    push("ysum", 2, vpart.at[1, rows((1 - yh) * 192, 192)], y_in, yp)
    push("vin", 0, orbitals.at[other_rows], field.at[0, core], partner)
    lax.fori_loop(0, 4, couplings, 0)
    couple_first(0)
    couple_first(1)
    ring_second(0)
    ring_second(1)
    arrive("ysum", 2, y_in)
    mine = rows(yh * 192, 192)
    vpart[1, mine, :] = vpart[1, mine, :] + y_in[...]
    ring_first(2)
    couple_third(0)
    couple_third(1)
    ring_second(2)
    couple_fourth(0)
    ring_last(2, vblock)
    for s in range(2):
        share("vx", s, vblock, chunk(2, x, s), xm)
        share("vx", 2 + s, vblock, chunk(2, x, s), xp)
    share("vy", 0, vblock, strip(x, yh), yp)
    couple_fourth(1)
    couple_forward(0, yh)
    for s in range(2):
        where = chunk(2, x + 1 + 2 * s, s)
        arrive("vx", 3 * s, vblock.at[where])
        share("vf", s, vblock, where, (xm, xp)[s])
    arrive("vx", 1, vblock.at[chunk(2, x + 1, 1)])
    arrive("vx", 2, vblock.at[chunk(2, x + 3, 0)])
    share("vy", 1, vblock, strip(x + 1, yh), yp)
    share("vy", 2, vblock, strip(x + 3, yh), yp)
    couple_fifth(0)
    couple_forward(1, yh)
    couple_fifth(1)
    for s in range(2):
        arrive("vf", s, vblock.at[chunk(2, x + 2, s)])
    share("vy", 3, vblock, strip(x + 2, yh), yp)
    couple_forward(0, 1 - yh)
    couple_forward(1, 1 - yh)

    for number, shift in ((0, 0), (1, 1), (2, 3), (3, 2)):
        arrive("vy", number, vblock.at[strip(x + shift, 1 - yh)])
    diagonal = jnp.where(
        lax.broadcasted_iota(jnp.int32, (128, 128), 0) == lax.broadcasted_iota(jnp.int32, (128, 128), 1), 4.0 / 12.0, 0.0
    )
    def halved(block):
        return (block + block.T) * (0.5 / 12.0) - diagonal

    def near_store(first, second, block):
        high, low = split(block)
        near_part[0, first : first + block.shape[0], second : second + block.shape[1]] = high
        near_part[1, first : first + block.shape[0], second : second + block.shape[1]] = low

    for k in range(2):
        first = k * 192
        corner = k * NB
        near_store(corner, corner, halved(vblock[first : first + 128, :128]))
        cross = vblock[first : first + 128, 128:] * (0.5 / 12.0)
        near_store(corner, corner + 128, cross)
        near_store(corner + 128, corner, cross.T)
        last = jnp.concatenate([vblock[first + 128 : first + 192, :128], vblock[first + 128 : first + 192, 128:]], axis=0)
        near_store(corner + 128, corner + 128, halved(last))
    couple_end(0)
    couple_end(1)
    block = cblock[NB:, :] * (1.0 / 12.0)
    high, low = split(block)
    down_part[0] = high
    down_part[1] = low
    high, low = split(block.T)
    up_part[0] = high
    up_part[1] = low
    block = cblock[:NB, :] * (1.0 / 12.0)
    near_store(0, NB, block)
    near_store(NB, 0, block.T)
    own_field.wait()
    arrive("vin", 0, field.at[0, other])

    def doubled(value):
        high, low = split(value)
        return jnp.concatenate([high, low], axis=1)

    def times(matrix, pair):
        both = nn(matrix[0], pair)
        return both[:, :128] + (both[:, 128:] + nn(matrix[1], pair[:, :128]))

    def halo(name, n, j):
        if name == "up":
            return remote("up", n * 2 + j, up_out.at[n, j], up_in.at[n, j], after)
        return remote("down", n * 2 + j, field.at[n, j, pl.ds(0, 256)], down_in.at[n, j], before)

    def filter_step(m, carry):
        n = jnp.maximum(m - 1, 0)
        oldest = jnp.maximum(m - 2, 0)
        scale = jnp.where(m == 1, 1.0, 2.0)
        keep = jnp.where(m == 1, 0.0, 1.0)

        @pl.when(m > 0)
        def _():
            parts = [split(field[n, j]) for j in range(2)]
            high = jnp.concatenate([parts[0][0], parts[1][0]], axis=1)
            low = jnp.concatenate([parts[0][1], parts[1][1]], axis=1)
            near_sum[...] = nn(near_part[0], high) + (nn(near_part[0], low) + nn(near_part[1], high))

        def column_step(j, inner):
            lanes = pl.ds(pl.multiple_of(j * 128, 128), 128)

            @pl.when(m > 0)
            def _():
                halo("up", n, j).wait_recv()
                value = scale * (near_sum[:256, lanes] + up_in[n, j])
                field[m, j, :256, :] = value - keep * field[oldest, j, :256, :]

            @pl.when(m < 4)
            def _():
                halo("down", m, j).start()

            @pl.when(m > 0)
            def _():
                halo("down", n, j).wait_recv()
                value = scale * (near_sum[256:, lanes] + times(down_part, doubled(down_in[n, j])))
                field[m, j, 256:, :] = value - keep * field[oldest, j, 256:, :]

            @pl.when(m < 4)
            def _():
                up_out[m, j] = times(up_part, doubled(field[m, j, 256:, :]))
                halo("up", m, j).start()

            @pl.when((m == 4) & (j == other))
            def _():
                remote("vout", 0, field.at[4, other], out.at[own_rows], partner).start()

            return inner

        return lax.fori_loop(0, 2, column_step, carry)

    lax.fori_loop(0, 5, filter_step, 0)
    out[own_rows, :] = field[4, core]

    def drain(k, carry):
        n, j = k // 2, lax.rem(k, 2)
        halo("up", n, j).wait_send()
        halo("down", n, j).wait_send()
        return carry

    lax.fori_loop(0, 8, drain, 0)
    for copy in started:
        copy.wait_send()
    sent("lead", 0, tl.at[0])
    sent("pair", 0, vpart.at[0])
    for unit in range(2):
        sent("pair", 1 + unit, cpart.at[0, rows(unit * NB, NB)])
    sent("vout", 0, field.at[4, other])
    arrive("vout", 0, out.at[other_rows])


def body(basis, applied, quad, face_index, face_pairing, orbitals):
    anywhere = pl.BlockSpec(memory_space=pl.ANY)
    return pl.pallas_call(
        kernel,
        out_shape=pltpu.VMEM(orbitals.shape, F32),
        in_specs=[anywhere] * 6,
        out_specs=pl.BlockSpec(memory_space=pltpu.VMEM),
        scratch_shapes=[
            pltpu.VMEM((4, 512, NB), F32),
            pltpu.VMEM((4, 512, NB), F32),
            pltpu.VMEM(quad.shape, F32),
            pltpu.VMEM(face_index.shape, jnp.int32),
            pltpu.VMEM(face_pairing.shape, jnp.int32),
            pltpu.VMEM((2, 4, NB, 512), BF16),
            pltpu.VMEM((4, NB, 128), F32),
            pltpu.VMEM((4, NB, 128), F32),
            pltpu.VMEM((5, NB, 128), F32),
            pltpu.VMEM((2, 384, NB), F32),
            pltpu.VMEM((2, 512, NB), F32),
            pltpu.VMEM((384, NB), F32),
            pltpu.VMEM((512, NB), F32),
            pltpu.VMEM((6, 24, NB), F32),
            pltpu.VMEM((2, 6, 32, NB), F32),
            pltpu.VMEM((192, NB), F32),
            pltpu.VMEM((2, 32, NB), F32),
            pltpu.VMEM((384, NB), F32),
            pltpu.VMEM((512, NB), F32),
            pltpu.VMEM((2, 512, 512), BF16),
            pltpu.VMEM((2, NB, NB), BF16),
            pltpu.VMEM((2, NB, NB), BF16),
            pltpu.VMEM((5, 2, 512, 128), F32),
            pltpu.VMEM((512, NB), F32),
            pltpu.VMEM((4, 2, NB, 128), F32),
            pltpu.VMEM((4, 2, NB, 128), F32),
            pltpu.VMEM((4, 2, NB, 128), F32),
            pltpu.SemaphoreType.DMA((12,)),
            pltpu.SemaphoreType.DMA((COPIES,)),
            pltpu.SemaphoreType.DMA((COPIES,)),
        ],
        name="filtered",
        compiler_params=pltpu.CompilerParams(collective_id=0, has_side_effects=True),
    )(basis, applied, quad, face_index, face_pairing, orbitals)


def solution(mesh):
    return jax.shard_map(
        body,
        mesh=mesh,
        in_specs=(
            P("elem", "pts", None),
            P("elem", "pts", None),
            P("elem", "pts"),
            P("elem", None, "pts"),
            P("elem", "pts"),
            P("elem", "pts"),
        ),
        out_specs=P("elem", "pts"),
        check_vma=False,
    )
```

```python
import jax
import jax.numpy as jnp
from jax import lax
from jax.experimental import pallas as pl
from jax.experimental.pallas import tpu as pltpu
from jax.sharding import PartitionSpec as P

NB = 256
MESH = pl.DeviceIdType.MESH
NEAR = ((2, 1), (1, 1), (3, 1), (2, 0), (0, 1), (1, 0), (3, 0))
F32 = jnp.float32
BF16 = jnp.bfloat16


def split(value):
    high = value.astype(BF16)
    low = (value - high.astype(F32)).astype(BF16)
    return high, low


def nn(left, right):
    return lax.dot_general(left, right, (((1,), (0,)), ((), ())), preferred_element_type=F32)


def nt(left, right):
    return lax.dot_general(left, right, (((1,), (1,)), ((), ())), preferred_element_type=F32)


def three(product, left, right):
    return product(left[0], right[0]) + (product(left[0], right[1]) + product(left[1], right[0]))


class Slots:
    def __init__(self):
        self.count = 0

    def take(self, number=1):
        first = self.count
        self.count += number
        return first


def layout():
    slots = Slots()
    table = {}
    for name, number in (
        ("lead", 1), ("vin", 1), ("vout", 1), ("pair", 3), ("scatter", 21), ("gather", 21), ("up", 8), ("down", 8),
    ):
        table[name] = slots.take(number)
    return table, slots.count


TABLE, COPIES = layout()


def kernel(
    basis, applied, quad_in, index_in, pairing_in, orbitals, out,
    b_buf, a_buf, quad, face_index, face_pairing, bq, ta, tb, tl, vpart, cpart, vpair, cpair, v_in, c_in, vblock, cblock,
    near_part, up_part, down_part, field, near_sum, up_out, up_in, down_in,
    local, send, recv,
):
    elem = lax.axis_index("elem")
    pts = lax.axis_index("pts")
    core = lax.rem(pts, 2)
    x = lax.rem(pts // 2, 4)
    yh = pts // 8
    other = 1 - core

    def at(elem_to, yh_to, x_to, core_to):
        return {"elem": lax.rem(elem_to, 16), "pts": yh_to * 8 + lax.rem(x_to, 4) * 2 + core_to}

    partner = at(elem, yh, x, other)
    chips = [(lax.rem(x + dx, 4), yh if dy == 0 else 1 - yh) for dx, dy in NEAR]
    peers = [at(elem, half, t, core) for t, half in chips]
    after = at(elem + core, yh, x, other)
    before = at(elem + 15 + core, yh, x, other)
    far = at(elem + 15 + 2 * core, yh, x, other)
    em = at(elem + 15, yh, x, core)
    ep = at(elem + 1, yh, x, core)

    started = []

    def remote(name, offset, source, target, device):
        index = TABLE[name] + offset
        return pltpu.make_async_remote_copy(
            src_ref=source, dst_ref=target, send_sem=send.at[index], recv_sem=recv.at[index],
            device_id=device, device_id_type=MESH,
        )

    def push(name, offset, source, target, device):
        copy = remote(name, offset, source, target, device)
        copy.start()
        started.append(copy)

    def arrive(name, offset, target):
        remote(name, offset, target, target, partner).wait_recv()

    def sent(name, offset, source):
        remote(name, offset, source, source, partner).wait_send()

    small = [
        pltpu.make_async_copy(index_in, face_index, local.at[9]),
        pltpu.make_async_copy(quad_in, quad, local.at[10]),
        pltpu.make_async_copy(pairing_in, face_pairing, local.at[11]),
    ]
    for copy in small:
        copy.start()
    for e in range(4):
        pltpu.make_async_copy(basis.at[e], b_buf.at[e], local.at[e]).start()
    own_rows = pl.ds(pl.multiple_of(core * 512, 512), 512)
    other_rows = pl.ds(pl.multiple_of(other * 512, 512), 512)
    own_field = pltpu.make_async_copy(orbitals.at[own_rows], field.at[0, core], local.at[8])

    barrier = pltpu.get_barrier_semaphore()
    for device in [partner, far, em, ep] + peers:
        pl.semaphore_signal(barrier, inc=1, device_id=device, device_id_type=MESH)

    point = lax.broadcasted_iota(jnp.int32, (512, NB), 0)
    lane = lax.broadcasted_iota(jnp.int32, (NB, 128), 1)

    def traces(e, carry):
        pltpu.make_async_copy(basis.at[e], b_buf.at[e], local.at[e]).wait()

        @pl.when(e == 0)
        def _():
            for copy in small:
                copy.wait()

        later = lax.rem(e + 2 * other, 4)
        pltpu.make_async_copy(applied.at[later], a_buf.at[later], local.at[4 + later]).start()
        turned = b_buf[e].T
        high, low = split(turned)
        picks = jnp.concatenate([face_index[e, r : r + 1, :] for r in (0, 2, 1, 3)], axis=1)
        chosen = jnp.where(point == picks, 1.0, 0.0).astype(BF16)
        values = nn(high, chosen) + nn(low, chosen)
        faces, inside = values[:, :128], values[:, 128:]
        ta[e] = faces
        tb[e] = inside
        tl[e] = jnp.where(lane < 64, faces, pltpu.roll(inside, 64, 1))
        high, low = split(turned * quad[pl.ds(e, 1), :])
        bq[0, e] = high
        bq[1, e] = low
        return carry

    def rows(first, size):
        return pl.ds(pl.multiple_of(first, 8), size)

    def volumes(i, carry):
        e = lax.rem(i + 2 * other, 4)
        half = i // 2
        first = lax.rem(i, 2) * 192
        pltpu.make_async_copy(applied.at[e], a_buf.at[e], local.at[4 + e]).wait()
        faces = ta[e]
        total = three(nn, (bq[0, e], bq[1, e]), split(a_buf[e]))
        total = total + three(nt, split((2.0 * faces + tb[e]) * (1.0 / 1024.0)), split(faces))
        vpart[half, rows(first, 128), :128] = total[:128, :128]
        vpart[half, rows(first, 128), 128:] = total[:128, 128:] + total[128:, :128].T
        vpart[half, rows(first + 128, 64), :128] = total[128:192, 128:]
        vpart[half, rows(first + 128, 64), 128:] = total[192:, 128:]

        @pl.when((i == 1) & (depth > 0))
        def _():
            remote("pair", 0, vpart.at[0], vpair, partner).start()

        return carry

    row = lax.broadcasted_iota(jnp.int32, (128, NB), 0)
    column = lax.broadcasted_iota(jnp.int32, (128, NB), 1)
    factor = jnp.where(
        column < 128,
        jnp.where(column < 64, 0.0, jnp.where(row < 64, -3.0, 0.5)),
        jnp.where(column < 192, 0.0, jnp.where(row < 64, -0.5, 0.0)),
    ) * (1.0 / 1024.0)
    slot = jnp.where(row < 64, row, row - 64)

    def couplings(i, carry):
        e = jnp.where((core == 1) | (i == 3), i, lax.rem(i + 2, 3))
        half = jnp.where(e // 2 == core, 1, 0)
        k = lax.rem(e, 2)

        @pl.when(i == 3)
        def _():
            arrive("lead", 0, tl.at[4])

        order = face_pairing[pl.ds(e, 1), :]
        order = jnp.concatenate([order] * 4, axis=1)
        mixing = jnp.where(slot == order, factor, 0.0).astype(BF16)
        high, low = split(jnp.concatenate([ta[e], tb[e]], axis=1))
        sides = nt(high, mixing) + nt(low, mixing)
        mine = rows(k * NB, NB)
        cpart[half, mine, :] = three(nt, split(sides), split(tl[e + 1]))

        @pl.when(half == 0)
        def _():
            remote("pair", 1 + k, cpart.at[0, mine], cpair.at[mine], partner).start()

        return carry

    sizes = (32, 32, 48)

    def chunk(unit, t, half):
        return rows(lax.rem(unit, 2) * NB + (half * 4 + t) * sizes[unit], sizes[unit])

    def sources(k):
        dx, dy = NEAR[k]
        return lax.rem(x + 4 - dx, 4), yh if dy == 0 else 1 - yh

    def arrived(unit, k):
        return v_in.at[k] if unit == 2 else c_in.at[unit, k]

    def part(unit):
        return vpart.at[1] if unit == 2 else cpart.at[1]

    def block(unit):
        return vblock if unit == 2 else cblock

    def scatter(unit):
        for k in range(7):
            push("scatter", unit * 7 + k, part(unit).at[chunk(unit, *chips[k])], arrived(unit, k), peers[k])

    def reduce(unit):
        where = chunk(unit, x, yh)
        total = part(unit)[where, :]
        for k in (6, 5, 4, 3, 2, 1, 0):
            arrive("scatter", unit * 7 + k, arrived(unit, k))
            total = total + arrived(unit, k)[...]
        block(unit)[where, :] = total

    def gather(unit):
        where = chunk(unit, x, yh)
        for k in range(7):
            push("gather", unit * 7 + k, block(unit).at[where], block(unit).at[where], peers[k])

    def gathered(unit):
        for k in (6, 5, 4, 3, 2, 1, 0):
            arrive("gather", unit * 7 + k, block(unit).at[chunk(unit, *sources(k))])

    def couple(unit):
        where = rows(unit * NB, NB)
        arrive("pair", 1 + unit, cpair.at[where])
        cpart[1, where, :] = cpart[1, where, :] + cpair[where, :]
        scatter(unit)

    def doubled(value):
        high, low = split(value)
        return jnp.concatenate([high, low], axis=1)

    def times(matrix, pair):
        both = nn(matrix[0], pair)
        return both[:, :128] + (both[:, 128:] + nn(matrix[1], pair[:, :128]))

    def halo(name, n, j):
        if name == "up":
            return remote("up", n * 2 + j, up_out.at[n, j], up_in.at[n, j], after)
        return remote("down", n * 2 + j, field.at[n, j, pl.ds(0, 256)], down_in.at[n, j], before)

    def offer_up(n, j):
        up_out[n, j] = times(up_part, doubled(field[n, j, 256:, :]))
        halo("up", n, j).start()

    def meet():
        pl.semaphore_wait(barrier, 11)
        remote("lead", 0, tl.at[0], tl.at[4], em).start()

    depth = lax.rem(elem, 8)
    lax.fori_loop(0, 4, traces, 0)
    pl.when(depth > 0)(meet)
    lax.fori_loop(0, 4, volumes, 0)
    @pl.when(depth == 0)
    def _():
        meet()
        remote("pair", 0, vpart.at[0], vpair, partner).start()

    arrive("pair", 0, vpair)
    vpart[1] = vpart[1] + vpair[...]
    scatter(2)
    own_field.start()
    push("vin", 0, orbitals.at[other_rows], field.at[0, core], partner)
    lax.fori_loop(0, 4, couplings, 0)
    couple(0)
    couple(1)
    reduce(2)
    gather(2)
    reduce(1)
    gather(1)
    reduce(0)
    gather(0)
    gathered(1)
    outer = cblock[NB:, :] * (1.0 / 12.0)
    high, low = split(outer.T)
    up_part[0] = high
    up_part[1] = low
    high, low = split(outer)
    down_part[0] = high
    down_part[1] = low
    own_field.wait()
    arrive("vin", 0, field.at[0, other])
    for j in range(2):
        halo("down", 0, j).start()
        offer_up(0, j)

    diagonal = jnp.where(
        lax.broadcasted_iota(jnp.int32, (128, 128), 0) == lax.broadcasted_iota(jnp.int32, (128, 128), 1), 4.0 / 12.0, 0.0
    )
    def halved(corner):
        return (corner + corner.T) * (0.5 / 12.0) - diagonal

    def near_store(first, second, value):
        high, low = split(value)
        near_part[0, first : first + value.shape[0], second : second + value.shape[1]] = high
        near_part[1, first : first + value.shape[0], second : second + value.shape[1]] = low

    gathered(2)
    for k in range(2):
        first = k * 192
        corner = k * NB
        near_store(corner, corner, halved(vblock[first : first + 128, :128]))
        cross = vblock[first : first + 128, 128:] * (0.5 / 12.0)
        near_store(corner, corner + 128, cross)
        near_store(corner + 128, corner, cross.T)
        last = jnp.concatenate([vblock[first + 128 : first + 192, :128], vblock[first + 128 : first + 192, 128:]], axis=0)
        near_store(corner + 128, corner + 128, halved(last))
    gathered(0)
    inner = cblock[:NB, :] * (1.0 / 12.0)
    near_store(0, NB, inner)
    near_store(NB, 0, inner.T)
    def filter_step(m, carry):
        n = m - 1
        oldest = jnp.maximum(m - 2, 0)
        scale = jnp.where(m == 1, 1.0, 2.0)
        keep = jnp.where(m == 1, 0.0, 1.0)
        parts = [split(field[n, j]) for j in range(2)]
        high = jnp.concatenate([parts[0][0], parts[1][0]], axis=1)
        low = jnp.concatenate([parts[0][1], parts[1][1]], axis=1)
        near_sum[...] = nn(near_part[0], high) + (nn(near_part[0], low) + nn(near_part[1], high))

        def column_step(j, inner):
            lanes = pl.ds(pl.multiple_of(j * 128, 128), 128)
            halo("up", n, j).wait_recv()
            value = scale * (near_sum[:256, lanes] + up_in[n, j])
            field[m, j, :256, :] = value - keep * field[oldest, j, :256, :]

            @pl.when(m < 4)
            def _():
                halo("down", m, j).start()

            halo("down", n, j).wait_recv()
            value = scale * (near_sum[256:, lanes] + times(down_part, doubled(down_in[n, j])))
            field[m, j, 256:, :] = value - keep * field[oldest, j, 256:, :]

            @pl.when(m < 4)
            def _():
                offer_up(m, j)

            @pl.when((m == 4) & (j == other))
            def _():
                remote("vout", 0, field.at[4, other], out.at[own_rows], partner).start()

            return inner

        return lax.fori_loop(0, 2, column_step, carry)

    lax.fori_loop(1, 5, filter_step, 0)
    out[own_rows, :] = field[4, core]

    def drain(k, carry):
        n, j = k // 2, lax.rem(k, 2)
        halo("up", n, j).wait_send()
        halo("down", n, j).wait_send()
        return carry

    lax.fori_loop(0, 8, drain, 0)
    for copy in started:
        copy.wait_send()
    sent("lead", 0, tl.at[0])
    sent("pair", 0, vpart.at[0])
    for unit in range(2):
        sent("pair", 1 + unit, cpart.at[0, rows(unit * NB, NB)])
    sent("vout", 0, field.at[4, other])
    arrive("vout", 0, out.at[other_rows])


def body(basis, applied, quad, face_index, face_pairing, orbitals):
    anywhere = pl.BlockSpec(memory_space=pl.ANY)
    return pl.pallas_call(
        kernel,
        out_shape=pltpu.VMEM(orbitals.shape, F32),
        in_specs=[anywhere] * 6,
        out_specs=pl.BlockSpec(memory_space=pltpu.VMEM),
        scratch_shapes=[
            pltpu.VMEM((4, 512, NB), F32),
            pltpu.VMEM((4, 512, NB), F32),
            pltpu.VMEM(quad.shape, F32),
            pltpu.VMEM(face_index.shape, jnp.int32),
            pltpu.VMEM(face_pairing.shape, jnp.int32),
            pltpu.VMEM((2, 4, NB, 512), BF16),
            pltpu.VMEM((4, NB, 128), F32),
            pltpu.VMEM((4, NB, 128), F32),
            pltpu.VMEM((5, NB, 128), F32),
            pltpu.VMEM((2, 384, NB), F32),
            pltpu.VMEM((2, 512, NB), F32),
            pltpu.VMEM((384, NB), F32),
            pltpu.VMEM((512, NB), F32),
            pltpu.VMEM((7, 48, NB), F32),
            pltpu.VMEM((2, 7, 32, NB), F32),
            pltpu.VMEM((384, NB), F32),
            pltpu.VMEM((512, NB), F32),
            pltpu.VMEM((2, 512, 512), BF16),
            pltpu.VMEM((2, NB, NB), BF16),
            pltpu.VMEM((2, NB, NB), BF16),
            pltpu.VMEM((5, 2, 512, 128), F32),
            pltpu.VMEM((512, NB), F32),
            pltpu.VMEM((4, 2, NB, 128), F32),
            pltpu.VMEM((4, 2, NB, 128), F32),
            pltpu.VMEM((4, 2, NB, 128), F32),
            pltpu.SemaphoreType.DMA((12,)),
            pltpu.SemaphoreType.DMA((COPIES,)),
            pltpu.SemaphoreType.DMA((COPIES,)),
        ],
        name="filtered",
        compiler_params=pltpu.CompilerParams(collective_id=0, has_side_effects=True),
    )(basis, applied, quad, face_index, face_pairing, orbitals)


def solution(mesh):
    return jax.shard_map(
        body,
        mesh=mesh,
        in_specs=(
            P("elem", "pts", None),
            P("elem", "pts", None),
            P("elem", "pts"),
            P("elem", None, "pts"),
            P("elem", "pts"),
            P("elem", "pts"),
        ),
        out_specs=P("elem", "pts"),
        check_vma=False,
    )
```

```python
import jax
import jax.numpy as jnp
from jax import lax
from jax.experimental import pallas as pl
from jax.experimental.pallas import tpu as pltpu
from jax.sharding import PartitionSpec as P

NB = 256
MESH = pl.DeviceIdType.MESH
NEAR = ((2, 1), (1, 1), (3, 1), (2, 0), (0, 1), (1, 0), (3, 0))
ROW = (3, 5, 6)
COLUMN = 4
ORDERS = ("direct", "direct", "yx")
F32 = jnp.float32
BF16 = jnp.bfloat16


def split(value):
    high = value.astype(BF16)
    low = (value - high.astype(F32)).astype(BF16)
    return high, low


def nn(left, right):
    return lax.dot_general(left, right, (((1,), (0,)), ((), ())), preferred_element_type=F32)


def nt(left, right):
    return lax.dot_general(left, right, (((1,), (1,)), ((), ())), preferred_element_type=F32)


def three(product, left, right):
    return product(left[0], right[0]) + (product(left[0], right[1]) + product(left[1], right[0]))


class Slots:
    def __init__(self):
        self.count = 0

    def take(self, number=1):
        first = self.count
        self.count += number
        return first


def layout():
    slots = Slots()
    table = {}
    for name, number in (
        ("lead", 1), ("vin", 1), ("vout", 1), ("pair", 3), ("scatter", 21), ("gather", 21), ("up", 8), ("down", 8),
    ):
        table[name] = slots.take(number)
    return table, slots.count


TABLE, COPIES = layout()


def kernel(
    basis, applied, quad_in, index_in, pairing_in, orbitals, out,
    b_buf, a_buf, quad, face_index, face_pairing, bq, ta, tb, tl, vpart, cpart, vpair, cpair, v_in, c_in, vblock, cblock,
    near_part, up_part, down_part, field, near_sum, up_out, up_in, down_in,
    local, send, recv,
):
    elem = lax.axis_index("elem")
    pts = lax.axis_index("pts")
    core = lax.rem(pts, 2)
    x = lax.rem(pts // 2, 4)
    yh = pts // 8
    other = 1 - core

    def at(elem_to, yh_to, x_to, core_to):
        return {"elem": lax.rem(elem_to, 16), "pts": yh_to * 8 + lax.rem(x_to, 4) * 2 + core_to}

    partner = at(elem, yh, x, other)
    chips = [(lax.rem(x + dx, 4), yh if dy == 0 else 1 - yh) for dx, dy in NEAR]
    peers = [at(elem, half, t, core) for t, half in chips]
    after = at(elem + core, yh, x, other)
    before = at(elem + 15 + core, yh, x, other)
    far = at(elem + 15 + 2 * core, yh, x, other)
    em = at(elem + 15, yh, x, core)
    ep = at(elem + 1, yh, x, core)

    started = []

    def remote(name, offset, source, target, device):
        index = TABLE[name] + offset
        return pltpu.make_async_remote_copy(
            src_ref=source, dst_ref=target, send_sem=send.at[index], recv_sem=recv.at[index],
            device_id=device, device_id_type=MESH,
        )

    def push(name, offset, source, target, device):
        copy = remote(name, offset, source, target, device)
        copy.start()
        started.append(copy)

    def arrive(name, offset, target):
        remote(name, offset, target, target, partner).wait_recv()

    def sent(name, offset, source):
        remote(name, offset, source, source, partner).wait_send()

    small = [
        pltpu.make_async_copy(index_in, face_index, local.at[9]),
        pltpu.make_async_copy(quad_in, quad, local.at[10]),
        pltpu.make_async_copy(pairing_in, face_pairing, local.at[11]),
    ]
    for copy in small:
        copy.start()
    for e in range(4):
        pltpu.make_async_copy(basis.at[e], b_buf.at[e], local.at[e]).start()
    own_rows = pl.ds(pl.multiple_of(core * 512, 512), 512)
    other_rows = pl.ds(pl.multiple_of(other * 512, 512), 512)
    own_field = pltpu.make_async_copy(orbitals.at[own_rows], field.at[0, core], local.at[8])
    own_field.start()

    barrier = pltpu.get_barrier_semaphore()
    for device in [partner, far, em, ep] + peers:
        pl.semaphore_signal(barrier, inc=1, device_id=device, device_id_type=MESH)

    point = lax.broadcasted_iota(jnp.int32, (512, NB), 0)
    lane = lax.broadcasted_iota(jnp.int32, (NB, 128), 1)

    def trace_pair(k, carry):
        @pl.when(k == 0)
        def _():
            for copy in small:
                copy.wait()

        for e in (2 * k, 2 * k + 1):
            later = lax.rem(e + 2 * other, 4)
            pltpu.make_async_copy(basis.at[e], b_buf.at[e], local.at[e]).wait()
            pltpu.make_async_copy(applied.at[later], a_buf.at[later], local.at[4 + later]).start()
        traces(2 * k)
        traces(2 * k + 1)
        return carry

    def traces(e):
        turned = b_buf[e].T
        high, low = split(turned)
        picks = jnp.concatenate([face_index[e, r : r + 1, :] for r in (0, 2, 1, 3)], axis=1)
        chosen = jnp.where(point == picks, 1.0, 0.0).astype(BF16)
        values = nn(high, chosen) + nn(low, chosen)
        faces, inside = values[:, :128], values[:, 128:]
        ta[e] = faces
        tb[e] = inside
        tl[e] = jnp.where(lane < 64, faces, pltpu.roll(inside, 64, 1))
        high, low = split(turned * quad[pl.ds(e, 1), :])
        bq[0, e] = high
        bq[1, e] = low

    def rows(first, size):
        return pl.ds(pl.multiple_of(first, 8), size)

    def volume_pair(half, carry):
        for k in range(2):
            e = lax.rem(2 * half + k + 2 * other, 4)
            pltpu.make_async_copy(applied.at[e], a_buf.at[e], local.at[4 + e]).wait()
        volumes(half, 0)
        volumes(half, 1)

        @pl.when((half == 0) & (depth > 0))
        def _():
            remote("pair", 0, vpart.at[0], vpair, partner).start()

        return carry

    def volumes(half, k):
        e = lax.rem(2 * half + k + 2 * other, 4)
        first = k * 192
        faces = ta[e]
        total = three(nn, (bq[0, e], bq[1, e]), split(a_buf[e]))
        total = total + three(nt, split((2.0 * faces + tb[e]) * (1.0 / 1024.0)), split(faces))
        vpart[half, rows(first, 128), :128] = total[:128, :128]
        vpart[half, rows(first, 128), 128:] = total[:128, 128:] + total[128:, :128].T
        vpart[half, rows(first + 128, 64), :128] = total[128:192, 128:]
        vpart[half, rows(first + 128, 64), 128:] = total[192:, 128:]

    row = lax.broadcasted_iota(jnp.int32, (128, NB), 0)
    column = lax.broadcasted_iota(jnp.int32, (128, NB), 1)
    factor = jnp.where(
        column < 128,
        jnp.where(column < 64, 0.0, jnp.where(row < 64, -3.0, 0.5)),
        jnp.where(column < 192, 0.0, jnp.where(row < 64, -0.5, 0.0)),
    ) * (1.0 / 1024.0)
    slot = jnp.where(row < 64, row, row - 64)

    def couplings(i, carry):
        e = jnp.where((core == 1) | (i == 3), i, lax.rem(i + 2, 3))
        half = jnp.where(e // 2 == core, 1, 0)
        k = lax.rem(e, 2)

        @pl.when(i == 3)
        def _():
            arrive("lead", 0, tl.at[4])

        order = face_pairing[pl.ds(e, 1), :]
        order = jnp.concatenate([order] * 4, axis=1)
        mixing = jnp.where(slot == order, factor, 0.0).astype(BF16)
        high, low = split(jnp.concatenate([ta[e], tb[e]], axis=1))
        sides = nt(high, mixing) + nt(low, mixing)
        mine = rows(k * NB, NB)
        cpart[half, mine, :] = three(nt, split(sides), split(tl[e + 1]))

        @pl.when(half == 0)
        def _():
            remote("pair", 1 + k, cpart.at[0, mine], cpair.at[mine], partner).start()

        return carry

    sizes = (32, 32, 48)

    def chunk(unit, t, half):
        return rows(lax.rem(unit, 2) * NB + (half * 4 + t) * sizes[unit], sizes[unit])

    def sources(k):
        dx, dy = NEAR[k]
        return lax.rem(x + 4 - dx, 4), yh if dy == 0 else 1 - yh

    def arrived(unit, k):
        return v_in.at[k] if unit == 2 else c_in.at[unit, k]

    def part(unit):
        return vpart.at[1] if unit == 2 else cpart.at[1]

    def block(unit):
        return vblock if unit == 2 else cblock

    def scatter(unit):
        for k in range(7):
            push("scatter", unit * 7 + k, part(unit).at[chunk(unit, *chips[k])], arrived(unit, k), peers[k])

    def reduce(unit):
        where = chunk(unit, x, yh)
        total = part(unit)[where, :]
        for k in (6, 5, 4, 3, 2, 1, 0):
            arrive("scatter", unit * 7 + k, arrived(unit, k))
            total = total + arrived(unit, k)[...]
        block(unit)[where, :] = total

    def share(unit, slot, where, k):
        push("gather", unit * 7 + slot, block(unit).at[where], block(unit).at[where], peers[k])

    def gather(unit):
        where = chunk(unit, x, yh)
        if ORDERS[unit] == "direct":
            for k in range(7):
                share(unit, k, where, k)
            return
        for i, k in enumerate(ROW):
            share(unit, 1 + i, where, k)
        share(unit, 0, where, COLUMN)

    def forward(unit):
        if ORDERS[unit] == "yx":
            where = chunk(unit, x, 1 - yh)
            arrive("gather", unit * 7, block(unit).at[where])
            for i, k in enumerate(ROW):
                share(unit, 4 + i, where, k)
        if ORDERS[unit] == "xy":
            for i in (2, 1, 0):
                where = chunk(unit, sources(ROW[i])[0], yh)
                arrive("gather", unit * 7 + 1 + i, block(unit).at[where])
                share(unit, 4 + i, where, COLUMN)

    def gathered(unit):
        if ORDERS[unit] == "direct":
            for k in (6, 5, 4, 3, 2, 1, 0):
                arrive("gather", unit * 7 + k, block(unit).at[chunk(unit, *sources(k))])
            return
        for i, k in enumerate(ROW):
            t, _ = sources(k)
            if ORDERS[unit] == "yx":
                arrive("gather", unit * 7 + 1 + i, block(unit).at[chunk(unit, t, yh)])
            arrive("gather", unit * 7 + 4 + i, block(unit).at[chunk(unit, t, 1 - yh)])
        if ORDERS[unit] == "xy":
            arrive("gather", unit * 7, block(unit).at[chunk(unit, x, 1 - yh)])

    def couple(unit):
        where = rows(unit * NB, NB)
        arrive("pair", 1 + unit, cpair.at[where])
        cpart[1, where, :] = cpart[1, where, :] + cpair[where, :]
        scatter(unit)

    def doubled(value):
        high, low = split(value)
        return jnp.concatenate([high, low], axis=1)

    def times(matrix, pair):
        both = nn(matrix[0], pair)
        return both[:, :128] + (both[:, 128:] + nn(matrix[1], pair[:, :128]))

    def halo(name, n, j):
        if name == "up":
            return remote("up", n * 2 + j, up_out.at[n, j], up_in.at[n, j], after)
        return remote("down", n * 2 + j, field.at[n, j, pl.ds(0, 256)], down_in.at[n, j], before)

    def offer_up(n, j):
        up_out[n, j] = times(up_part, doubled(field[n, j, 256:, :]))
        halo("up", n, j).start()

    def meet():
        pl.semaphore_wait(barrier, 11)
        remote("lead", 0, tl.at[0], tl.at[4], em).start()
        remote("vin", 0, orbitals.at[other_rows], field.at[0, core], partner).start()

    depth = lax.rem(elem, 8)
    lax.fori_loop(0, 2, trace_pair, 0)
    pl.when(depth > 0)(meet)
    lax.fori_loop(0, 2, volume_pair, 0)
    @pl.when(depth == 0)
    def _():
        meet()
        remote("pair", 0, vpart.at[0], vpair, partner).start()

    arrive("pair", 0, vpair)
    vpart[1] = vpart[1] + vpair[...]
    scatter(2)
    lax.fori_loop(0, 4, couplings, 0)
    couple(0)
    couple(1)
    reduce(2)
    gather(2)
    reduce(1)
    gather(1)
    reduce(0)
    gather(0)
    forward(2)
    forward(1)
    forward(0)
    gathered(1)
    outer = cblock[NB:, :] * (1.0 / 12.0)
    high, low = split(outer.T)
    up_part[0] = high
    up_part[1] = low
    high, low = split(outer)
    down_part[0] = high
    down_part[1] = low
    own_field.wait()
    arrive("vin", 0, field.at[0, other])
    for j in range(2):
        halo("down", 0, j).start()
        offer_up(0, j)

    diagonal = jnp.where(
        lax.broadcasted_iota(jnp.int32, (128, 128), 0) == lax.broadcasted_iota(jnp.int32, (128, 128), 1), 4.0 / 12.0, 0.0
    )
    def halved(corner):
        return (corner + corner.T) * (0.5 / 12.0) - diagonal

    def near_store(first, second, value):
        high, low = split(value)
        near_part[0, first : first + value.shape[0], second : second + value.shape[1]] = high
        near_part[1, first : first + value.shape[0], second : second + value.shape[1]] = low

    gathered(2)
    for k in range(2):
        first = k * 192
        corner = k * NB
        near_store(corner, corner, halved(vblock[first : first + 128, :128]))
        cross = vblock[first : first + 128, 128:] * (0.5 / 12.0)
        near_store(corner, corner + 128, cross)
        near_store(corner + 128, corner, cross.T)
        last = jnp.concatenate([vblock[first + 128 : first + 192, :128], vblock[first + 128 : first + 192, 128:]], axis=0)
        near_store(corner + 128, corner + 128, halved(last))
    gathered(0)
    inner = cblock[:NB, :] * (1.0 / 12.0)
    near_store(0, NB, inner)
    near_store(NB, 0, inner.T)
    def filter_step(m, carry):
        n = m - 1
        oldest = jnp.maximum(m - 2, 0)
        scale = jnp.where(m == 1, 1.0, 2.0)
        keep = jnp.where(m == 1, 0.0, 1.0)
        parts = [split(field[n, j]) for j in range(2)]
        high = jnp.concatenate([parts[0][0], parts[1][0]], axis=1)
        low = jnp.concatenate([parts[0][1], parts[1][1]], axis=1)
        near_sum[...] = nn(near_part[0], high) + (nn(near_part[0], low) + nn(near_part[1], high))

        def column_step(j, inner):
            lanes = pl.ds(pl.multiple_of(j * 128, 128), 128)
            halo("up", n, j).wait_recv()
            value = scale * (near_sum[:256, lanes] + up_in[n, j])
            field[m, j, :256, :] = value - keep * field[oldest, j, :256, :]

            @pl.when(m < 4)
            def _():
                halo("down", m, j).start()

            halo("down", n, j).wait_recv()
            value = scale * (near_sum[256:, lanes] + times(down_part, doubled(down_in[n, j])))
            field[m, j, 256:, :] = value - keep * field[oldest, j, 256:, :]

            @pl.when(m < 4)
            def _():
                offer_up(m, j)

            @pl.when((m == 4) & (j == other))
            def _():
                remote("vout", 0, field.at[4, other], out.at[own_rows], partner).start()

            return inner

        return lax.fori_loop(0, 2, column_step, carry)

    lax.fori_loop(1, 5, filter_step, 0)
    out[own_rows, :] = field[4, core]

    def drain(k, carry):
        n, j = k // 2, lax.rem(k, 2)
        halo("up", n, j).wait_send()
        halo("down", n, j).wait_send()
        return carry

    lax.fori_loop(0, 8, drain, 0)
    for copy in started:
        copy.wait_send()
    sent("lead", 0, tl.at[0])
    sent("vin", 0, field.at[0, core])
    sent("pair", 0, vpart.at[0])
    for unit in range(2):
        sent("pair", 1 + unit, cpart.at[0, rows(unit * NB, NB)])
    sent("vout", 0, field.at[4, other])
    arrive("vout", 0, out.at[other_rows])


def body(basis, applied, quad, face_index, face_pairing, orbitals):
    anywhere = pl.BlockSpec(memory_space=pl.ANY)
    return pl.pallas_call(
        kernel,
        out_shape=pltpu.VMEM(orbitals.shape, F32),
        in_specs=[anywhere] * 6,
        out_specs=pl.BlockSpec(memory_space=pltpu.VMEM),
        scratch_shapes=[
            pltpu.VMEM((4, 512, NB), F32),
            pltpu.VMEM((4, 512, NB), F32),
            pltpu.VMEM(quad.shape, F32),
            pltpu.VMEM(face_index.shape, jnp.int32),
            pltpu.VMEM(face_pairing.shape, jnp.int32),
            pltpu.VMEM((2, 4, NB, 512), BF16),
            pltpu.VMEM((4, NB, 128), F32),
            pltpu.VMEM((4, NB, 128), F32),
            pltpu.VMEM((5, NB, 128), F32),
            pltpu.VMEM((2, 384, NB), F32),
            pltpu.VMEM((2, 512, NB), F32),
            pltpu.VMEM((384, NB), F32),
            pltpu.VMEM((512, NB), F32),
            pltpu.VMEM((7, 48, NB), F32),
            pltpu.VMEM((2, 7, 32, NB), F32),
            pltpu.VMEM((384, NB), F32),
            pltpu.VMEM((512, NB), F32),
            pltpu.VMEM((2, 512, 512), BF16),
            pltpu.VMEM((2, NB, NB), BF16),
            pltpu.VMEM((2, NB, NB), BF16),
            pltpu.VMEM((5, 2, 512, 128), F32),
            pltpu.VMEM((512, NB), F32),
            pltpu.VMEM((4, 2, NB, 128), F32),
            pltpu.VMEM((4, 2, NB, 128), F32),
            pltpu.VMEM((4, 2, NB, 128), F32),
            pltpu.SemaphoreType.DMA((12,)),
            pltpu.SemaphoreType.DMA((COPIES,)),
            pltpu.SemaphoreType.DMA((COPIES,)),
        ],
        name="filtered",
        compiler_params=pltpu.CompilerParams(collective_id=0, has_side_effects=True),
    )(basis, applied, quad, face_index, face_pairing, orbitals)


def solution(mesh):
    return jax.shard_map(
        body,
        mesh=mesh,
        in_specs=(
            P("elem", "pts", None),
            P("elem", "pts", None),
            P("elem", "pts"),
            P("elem", None, "pts"),
            P("elem", "pts"),
            P("elem", "pts"),
        ),
        out_specs=P("elem", "pts"),
        check_vma=False,
    )
```

```python
import jax
import jax.numpy as jnp
from jax import lax
from jax.experimental import pallas as pl
from jax.experimental.pallas import tpu as pltpu
from jax.sharding import PartitionSpec as P

NB = 256
MESH = pl.DeviceIdType.MESH
NEAR = ((2, 1), (1, 1), (3, 1), (2, 0), (0, 1), (1, 0), (3, 0))
ROW = (3, 5, 6)
COLUMN = 4
ORDERS = ("yx", "direct", "yx")
F32 = jnp.float32
BF16 = jnp.bfloat16


def split(value):
    high = value.astype(BF16)
    low = (value - high.astype(F32)).astype(BF16)
    return high, low


def nn(left, right):
    return lax.dot_general(left, right, (((1,), (0,)), ((), ())), preferred_element_type=F32)


def nt(left, right):
    return lax.dot_general(left, right, (((1,), (1,)), ((), ())), preferred_element_type=F32)


def three(product, left, right):
    return product(left[0], right[0]) + (product(left[0], right[1]) + product(left[1], right[0]))


class Slots:
    def __init__(self):
        self.count = 0

    def take(self, number=1):
        first = self.count
        self.count += number
        return first


def layout():
    slots = Slots()
    table = {}
    for name, number in (
        ("lead", 1), ("vin", 1), ("vout", 2), ("pair", 3), ("scatter", 21), ("gather", 21), ("up", 8), ("down", 8),
    ):
        table[name] = slots.take(number)
    return table, slots.count


TABLE, COPIES = layout()


def kernel(
    basis, applied, quad_in, index_in, pairing_in, orbitals, out,
    b_buf, a_buf, quad, face_index, face_pairing, bq, ta, tb, tl, vpart, cpart, vpair, cpair, v_in, c_in, vblock, cblock,
    near_part, up_part, down_part, field, near_sum, up_out, up_in, down_in,
    local, send, recv,
):
    elem = lax.axis_index("elem")
    pts = lax.axis_index("pts")
    core = lax.rem(pts, 2)
    x = lax.rem(pts // 2, 4)
    yh = pts // 8
    other = 1 - core

    def at(elem_to, yh_to, x_to, core_to):
        return {"elem": lax.rem(elem_to, 16), "pts": yh_to * 8 + lax.rem(x_to, 4) * 2 + core_to}

    partner = at(elem, yh, x, other)
    chips = [(lax.rem(x + dx, 4), yh if dy == 0 else 1 - yh) for dx, dy in NEAR]
    peers = [at(elem, half, t, core) for t, half in chips]
    after = at(elem + core, yh, x, other)
    before = at(elem + 15 + core, yh, x, other)
    far = at(elem + 15 + 2 * core, yh, x, other)
    em = at(elem + 15, yh, x, core)
    ep = at(elem + 1, yh, x, core)

    started = []

    def remote(name, offset, source, target, device):
        index = TABLE[name] + offset
        return pltpu.make_async_remote_copy(
            src_ref=source, dst_ref=target, send_sem=send.at[index], recv_sem=recv.at[index],
            device_id=device, device_id_type=MESH,
        )

    def push(name, offset, source, target, device):
        copy = remote(name, offset, source, target, device)
        copy.start()
        started.append(copy)

    def arrive(name, offset, target):
        remote(name, offset, target, target, partner).wait_recv()

    def sent(name, offset, source):
        remote(name, offset, source, source, partner).wait_send()

    small = [
        pltpu.make_async_copy(index_in, face_index, local.at[9]),
        pltpu.make_async_copy(quad_in, quad, local.at[10]),
        pltpu.make_async_copy(pairing_in, face_pairing, local.at[11]),
    ]
    for copy in small:
        copy.start()
    for e in range(4):
        pltpu.make_async_copy(basis.at[e], b_buf.at[e], local.at[e]).start()
    own_rows = pl.ds(pl.multiple_of(core * 512, 512), 512)
    other_rows = pl.ds(pl.multiple_of(other * 512, 512), 512)
    own_field = pltpu.make_async_copy(orbitals.at[own_rows], field.at[0, core], local.at[8])
    own_field.start()

    barrier = pltpu.get_barrier_semaphore()
    for device in [partner, far, em, ep] + peers:
        pl.semaphore_signal(barrier, inc=1, device_id=device, device_id_type=MESH)

    point = lax.broadcasted_iota(jnp.int32, (512, NB), 0)
    lane = lax.broadcasted_iota(jnp.int32, (NB, 128), 1)

    def trace_pair(k, carry):
        @pl.when(k == 0)
        def _():
            for copy in small:
                copy.wait()

        for e in (2 * k, 2 * k + 1):
            later = lax.rem(e + 2 * other, 4)
            pltpu.make_async_copy(basis.at[e], b_buf.at[e], local.at[e]).wait()
            pltpu.make_async_copy(applied.at[later], a_buf.at[later], local.at[4 + later]).start()
        traces(2 * k)
        traces(2 * k + 1)
        return carry

    def traces(e):
        turned = b_buf[e].T
        high, low = split(turned)
        picks = jnp.concatenate([face_index[e, r : r + 1, :] for r in (0, 2, 1, 3)], axis=1)
        chosen = jnp.where(point == picks, 1.0, 0.0).astype(BF16)
        values = nn(high, chosen) + nn(low, chosen)
        faces, inside = values[:, :128], values[:, 128:]
        ta[e] = faces
        tb[e] = inside
        tl[e] = jnp.where(lane < 64, faces, pltpu.roll(inside, 64, 1))
        high, low = split(turned * quad[pl.ds(e, 1), :])
        bq[0, e] = high
        bq[1, e] = low

    def rows(first, size):
        return pl.ds(pl.multiple_of(first, 8), size)

    def volume_pair(half, carry):
        for k in range(2):
            e = lax.rem(2 * half + k + 2 * other, 4)
            pltpu.make_async_copy(applied.at[e], a_buf.at[e], local.at[4 + e]).wait()
        volumes(half, 0)
        volumes(half, 1)

        @pl.when((half == 0) & (depth > 0))
        def _():
            remote("pair", 0, vpart.at[0], vpair, partner).start()

        return carry

    def volumes(half, k):
        e = lax.rem(2 * half + k + 2 * other, 4)
        first = k * 192
        faces = ta[e]
        total = three(nn, (bq[0, e], bq[1, e]), split(a_buf[e]))
        total = total + three(nt, split((2.0 * faces + tb[e]) * (1.0 / 1024.0)), split(faces))
        vpart[half, rows(first, 128), :128] = total[:128, :128]
        vpart[half, rows(first, 128), 128:] = total[:128, 128:] + total[128:, :128].T
        vpart[half, rows(first + 128, 64), :128] = total[128:192, 128:]
        vpart[half, rows(first + 128, 64), 128:] = total[192:, 128:]

    row = lax.broadcasted_iota(jnp.int32, (128, NB), 0)
    column = lax.broadcasted_iota(jnp.int32, (128, NB), 1)
    factor = jnp.where(
        column < 128,
        jnp.where(column < 64, 0.0, jnp.where(row < 64, -3.0, 0.5)),
        jnp.where(column < 192, 0.0, jnp.where(row < 64, -0.5, 0.0)),
    ) * (1.0 / 1024.0)
    slot = jnp.where(row < 64, row, row - 64)

    def couplings(i, carry):
        e = jnp.where((core == 1) | (i == 3), i, lax.rem(i + 2, 3))
        half = jnp.where(e // 2 == core, 1, 0)
        k = lax.rem(e, 2)

        @pl.when(i == 3)
        def _():
            arrive("lead", 0, tl.at[4])

        order = face_pairing[pl.ds(e, 1), :]
        order = jnp.concatenate([order] * 4, axis=1)
        mixing = jnp.where(slot == order, factor, 0.0).astype(BF16)
        high, low = split(jnp.concatenate([ta[e], tb[e]], axis=1))
        sides = nt(high, mixing) + nt(low, mixing)
        mine = rows(k * NB, NB)
        cpart[half, mine, :] = three(nt, split(sides), split(tl[e + 1]))

        @pl.when(half == 0)
        def _():
            remote("pair", 1 + k, cpart.at[0, mine], cpair.at[mine], partner).start()

        return carry

    sizes = (32, 32, 48)

    def chunk(unit, t, half):
        return rows(lax.rem(unit, 2) * NB + (half * 4 + t) * sizes[unit], sizes[unit])

    def sources(k):
        dx, dy = NEAR[k]
        return lax.rem(x + 4 - dx, 4), yh if dy == 0 else 1 - yh

    def arrived(unit, k):
        return v_in.at[k] if unit == 2 else c_in.at[unit, k]

    def part(unit):
        return vpart.at[1] if unit == 2 else cpart.at[1]

    def block(unit):
        return vblock if unit == 2 else cblock

    def scatter(unit):
        for k in range(7):
            push("scatter", unit * 7 + k, part(unit).at[chunk(unit, *chips[k])], arrived(unit, k), peers[k])

    def reduce(unit):
        where = chunk(unit, x, yh)
        total = part(unit)[where, :]
        for k in (6, 5, 4, 3, 2, 1, 0):
            arrive("scatter", unit * 7 + k, arrived(unit, k))
            total = total + arrived(unit, k)[...]
        block(unit)[where, :] = total

    def share(unit, slot, where, k):
        push("gather", unit * 7 + slot, block(unit).at[where], block(unit).at[where], peers[k])

    def gather(unit):
        where = chunk(unit, x, yh)
        if ORDERS[unit] == "direct":
            for k in range(7):
                share(unit, k, where, k)
            return
        for i, k in enumerate(ROW):
            share(unit, 1 + i, where, k)
        share(unit, 0, where, COLUMN)

    def forward(unit):
        if ORDERS[unit] == "yx":
            where = chunk(unit, x, 1 - yh)
            arrive("gather", unit * 7, block(unit).at[where])
            for i, k in enumerate(ROW):
                share(unit, 4 + i, where, k)
        if ORDERS[unit] == "xy":
            for i in (2, 1, 0):
                where = chunk(unit, sources(ROW[i])[0], yh)
                arrive("gather", unit * 7 + 1 + i, block(unit).at[where])
                share(unit, 4 + i, where, COLUMN)

    def gathered(unit):
        if ORDERS[unit] == "direct":
            for k in (6, 5, 4, 3, 2, 1, 0):
                arrive("gather", unit * 7 + k, block(unit).at[chunk(unit, *sources(k))])
            return
        for i, k in enumerate(ROW):
            t, _ = sources(k)
            if ORDERS[unit] == "yx":
                arrive("gather", unit * 7 + 1 + i, block(unit).at[chunk(unit, t, yh)])
            arrive("gather", unit * 7 + 4 + i, block(unit).at[chunk(unit, t, 1 - yh)])
        if ORDERS[unit] == "xy":
            arrive("gather", unit * 7, block(unit).at[chunk(unit, x, 1 - yh)])

    def couple(unit):
        where = rows(unit * NB, NB)
        arrive("pair", 1 + unit, cpair.at[where])
        cpart[1, where, :] = cpart[1, where, :] + cpair[where, :]
        scatter(unit)

    def doubled(value):
        high, low = split(value)
        return jnp.concatenate([high, low], axis=1)

    def times(matrix, pair):
        both = nn(matrix[0], pair)
        return both[:, :128] + (both[:, 128:] + nn(matrix[1], pair[:, :128]))

    def halo(name, n, j):
        if name == "up":
            return remote("up", n * 2 + j, up_out.at[n, j], up_in.at[n, j], after)
        return remote("down", n * 2 + j, field.at[n, j, pl.ds(0, 256)], down_in.at[n, j], before)

    def offer_up(n, j):
        up_out[n, j] = times(up_part, doubled(field[n, j, 256:, :]))
        halo("up", n, j).start()

    def meet():
        pl.semaphore_wait(barrier, 11)
        remote("lead", 0, tl.at[0], tl.at[4], em).start()
        remote("vin", 0, orbitals.at[other_rows], field.at[0, core], partner).start()

    depth = lax.rem(elem, 8)
    lax.fori_loop(0, 2, trace_pair, 0)
    pl.when(depth > 0)(meet)
    lax.fori_loop(0, 2, volume_pair, 0)
    @pl.when(depth == 0)
    def _():
        meet()
        remote("pair", 0, vpart.at[0], vpair, partner).start()

    arrive("pair", 0, vpair)
    vpart[1] = vpart[1] + vpair[...]
    scatter(2)
    lax.fori_loop(0, 4, couplings, 0)
    couple(0)
    couple(1)
    reduce(2)
    gather(2)
    reduce(1)
    gather(1)
    reduce(0)
    gather(0)
    forward(2)
    forward(1)
    forward(0)
    gathered(1)
    outer = cblock[NB:, :] * (1.0 / 12.0)
    high, low = split(outer.T)
    up_part[0] = high
    up_part[1] = low
    high, low = split(outer)
    down_part[0] = high
    down_part[1] = low
    own_field.wait()
    arrive("vin", 0, field.at[0, other])
    for j in range(2):
        halo("down", 0, j).start()
        offer_up(0, j)

    diagonal = jnp.where(
        lax.broadcasted_iota(jnp.int32, (128, 128), 0) == lax.broadcasted_iota(jnp.int32, (128, 128), 1), 4.0 / 12.0, 0.0
    )
    def halved(corner):
        return (corner + corner.T) * (0.5 / 12.0) - diagonal

    def near_store(first, second, value):
        high, low = split(value)
        near_part[0, first : first + value.shape[0], second : second + value.shape[1]] = high
        near_part[1, first : first + value.shape[0], second : second + value.shape[1]] = low

    gathered(2)
    for k in range(2):
        first = k * 192
        corner = k * NB
        near_store(corner, corner, halved(vblock[first : first + 128, :128]))
        cross = vblock[first : first + 128, 128:] * (0.5 / 12.0)
        near_store(corner, corner + 128, cross)
        near_store(corner + 128, corner, cross.T)
        last = jnp.concatenate([vblock[first + 128 : first + 192, :128], vblock[first + 128 : first + 192, 128:]], axis=0)
        near_store(corner + 128, corner + 128, halved(last))
    gathered(0)
    inner = cblock[:NB, :] * (1.0 / 12.0)
    near_store(0, NB, inner)
    near_store(NB, 0, inner.T)
    def hand_over(k):
        return remote("vout", k, field.at[4, other, pl.ds(k * NB, NB)], out.at[rows(core * 512 + k * NB, NB)], partner)

    def filter_step(m, carry):
        n = m - 1
        oldest = jnp.maximum(m - 2, 0)
        scale = jnp.where(m == 1, 1.0, 2.0)
        keep = jnp.where(m == 1, 0.0, 1.0)
        parts = [split(field[n, j]) for j in range(2)]
        high = jnp.concatenate([parts[0][0], parts[1][0]], axis=1)
        low = jnp.concatenate([parts[0][1], parts[1][1]], axis=1)
        near_sum[...] = nn(near_part[0], high) + (nn(near_part[0], low) + nn(near_part[1], high))

        def column_step(j, inner):
            lanes = pl.ds(pl.multiple_of(j * 128, 128), 128)
            halo("up", n, j).wait_recv()
            value = scale * (near_sum[:256, lanes] + up_in[n, j])
            field[m, j, :256, :] = value - keep * field[oldest, j, :256, :]

            @pl.when((m == 4) & (j == other))
            def _():
                hand_over(0).start()

            @pl.when(m < 4)
            def _():
                halo("down", m, j).start()

            halo("down", n, j).wait_recv()
            value = scale * (near_sum[256:, lanes] + times(down_part, doubled(down_in[n, j])))
            field[m, j, 256:, :] = value - keep * field[oldest, j, 256:, :]

            @pl.when(m < 4)
            def _():
                offer_up(m, j)

            @pl.when((m == 4) & (j == other))
            def _():
                hand_over(1).start()

            return inner

        return lax.fori_loop(0, 2, column_step, carry)

    lax.fori_loop(1, 5, filter_step, 0)
    out[own_rows, :] = field[4, core]

    def drain(k, carry):
        n, j = k // 2, lax.rem(k, 2)
        halo("up", n, j).wait_send()
        halo("down", n, j).wait_send()
        return carry

    lax.fori_loop(0, 8, drain, 0)
    for copy in started:
        copy.wait_send()
    sent("lead", 0, tl.at[0])
    sent("vin", 0, field.at[0, core])
    sent("pair", 0, vpart.at[0])
    for unit in range(2):
        sent("pair", 1 + unit, cpart.at[0, rows(unit * NB, NB)])
    for k in range(2):
        hand_over(k).wait_send()
        arrive("vout", k, out.at[rows(other * 512 + k * NB, NB)])


def body(basis, applied, quad, face_index, face_pairing, orbitals):
    anywhere = pl.BlockSpec(memory_space=pl.ANY)
    return pl.pallas_call(
        kernel,
        out_shape=pltpu.VMEM(orbitals.shape, F32),
        in_specs=[anywhere] * 6,
        out_specs=pl.BlockSpec(memory_space=pltpu.VMEM),
        scratch_shapes=[
            pltpu.VMEM((4, 512, NB), F32),
            pltpu.VMEM((4, 512, NB), F32),
            pltpu.VMEM(quad.shape, F32),
            pltpu.VMEM(face_index.shape, jnp.int32),
            pltpu.VMEM(face_pairing.shape, jnp.int32),
            pltpu.VMEM((2, 4, NB, 512), BF16),
            pltpu.VMEM((4, NB, 128), F32),
            pltpu.VMEM((4, NB, 128), F32),
            pltpu.VMEM((5, NB, 128), F32),
            pltpu.VMEM((2, 384, NB), F32),
            pltpu.VMEM((2, 512, NB), F32),
            pltpu.VMEM((384, NB), F32),
            pltpu.VMEM((512, NB), F32),
            pltpu.VMEM((7, 48, NB), F32),
            pltpu.VMEM((2, 7, 32, NB), F32),
            pltpu.VMEM((384, NB), F32),
            pltpu.VMEM((512, NB), F32),
            pltpu.VMEM((2, 512, 512), BF16),
            pltpu.VMEM((2, NB, NB), BF16),
            pltpu.VMEM((2, NB, NB), BF16),
            pltpu.VMEM((5, 2, 512, 128), F32),
            pltpu.VMEM((512, NB), F32),
            pltpu.VMEM((4, 2, NB, 128), F32),
            pltpu.VMEM((4, 2, NB, 128), F32),
            pltpu.VMEM((4, 2, NB, 128), F32),
            pltpu.SemaphoreType.DMA((12,)),
            pltpu.SemaphoreType.DMA((COPIES,)),
            pltpu.SemaphoreType.DMA((COPIES,)),
        ],
        name="filtered",
        compiler_params=pltpu.CompilerParams(collective_id=0, has_side_effects=True),
    )(basis, applied, quad, face_index, face_pairing, orbitals)


def solution(mesh):
    return jax.shard_map(
        body,
        mesh=mesh,
        in_specs=(
            P("elem", "pts", None),
            P("elem", "pts", None),
            P("elem", "pts"),
            P("elem", None, "pts"),
            P("elem", "pts"),
            P("elem", "pts"),
        ),
        out_specs=P("elem", "pts"),
        check_vma=False,
    )
```

```python
import jax
import jax.numpy as jnp
from jax import lax
from jax.experimental import pallas as pl
from jax.experimental.pallas import tpu as pltpu
from jax.sharding import PartitionSpec as P

NB = 256
MESH = pl.DeviceIdType.MESH
NEAR = ((2, 1), (1, 1), (3, 1), (2, 0), (0, 1), (1, 0), (3, 0))
ROW = (3, 5, 6)
COLUMN = 4
ORDERS = ("yx", "direct", "yx")
F32 = jnp.float32
BF16 = jnp.bfloat16


def split(value):
    high = value.astype(BF16)
    low = (value - high.astype(F32)).astype(BF16)
    return high, low


def nn(left, right):
    return lax.dot_general(left, right, (((1,), (0,)), ((), ())), preferred_element_type=F32)


def nt(left, right):
    return lax.dot_general(left, right, (((1,), (1,)), ((), ())), preferred_element_type=F32)


def three(product, left, right):
    return product(left[0], right[0]) + (product(left[0], right[1]) + product(left[1], right[0]))


class Slots:
    def __init__(self):
        self.count = 0

    def take(self, number=1):
        first = self.count
        self.count += number
        return first


def layout():
    slots = Slots()
    table = {}
    for name, number in (
        ("lead", 1), ("vin", 1), ("vout", 2), ("pair", 3), ("scatter", 21), ("gather", 21), ("up", 8), ("down", 8),
    ):
        table[name] = slots.take(number)
    return table, slots.count


TABLE, COPIES = layout()


def kernel(
    basis, applied, quad_in, index_in, pairing_in, orbitals, out,
    b_buf, a_buf, quad, face_index, face_pairing, bq, ta, tb, tl, vpart, cpart, vpair, cpair, v_in, c_in, vblock, cblock,
    near_part, up_part, down_part, field, near_sum, up_out, up_in, down_in,
    local, send, recv,
):
    elem = lax.axis_index("elem")
    pts = lax.axis_index("pts")
    core = lax.rem(pts, 2)
    x = lax.rem(pts // 2, 4)
    yh = pts // 8
    other = 1 - core

    def at(elem_to, yh_to, x_to, core_to):
        return {"elem": lax.rem(elem_to, 16), "pts": yh_to * 8 + lax.rem(x_to, 4) * 2 + core_to}

    partner = at(elem, yh, x, other)
    chips = [(lax.rem(x + dx, 4), yh if dy == 0 else 1 - yh) for dx, dy in NEAR]
    peers = [at(elem, half, t, core) for t, half in chips]
    after = at(elem + core, yh, x, other)
    before = at(elem + 15 + core, yh, x, other)
    far = at(elem + 15 + 2 * core, yh, x, other)
    em = at(elem + 15, yh, x, core)
    ep = at(elem + 1, yh, x, core)

    started = []

    def remote(name, offset, source, target, device):
        index = TABLE[name] + offset
        return pltpu.make_async_remote_copy(
            src_ref=source, dst_ref=target, send_sem=send.at[index], recv_sem=recv.at[index],
            device_id=device, device_id_type=MESH,
        )

    def push(name, offset, source, target, device):
        copy = remote(name, offset, source, target, device)
        copy.start()
        started.append(copy)

    def arrive(name, offset, target):
        remote(name, offset, target, target, partner).wait_recv()

    def sent(name, offset, source):
        remote(name, offset, source, source, partner).wait_send()

    small = [
        pltpu.make_async_copy(index_in, face_index, local.at[9]),
        pltpu.make_async_copy(quad_in, quad, local.at[10]),
        pltpu.make_async_copy(pairing_in, face_pairing, local.at[11]),
    ]
    for copy in small:
        copy.start()
    for e in range(4):
        pltpu.make_async_copy(basis.at[e], b_buf.at[e], local.at[e]).start()
    own_rows = pl.ds(pl.multiple_of(core * 512, 512), 512)
    other_rows = pl.ds(pl.multiple_of(other * 512, 512), 512)
    own_field = pltpu.make_async_copy(orbitals.at[own_rows], field.at[0, core], local.at[8])
    own_field.start()

    barrier = pltpu.get_barrier_semaphore()
    for device in [partner, far, em, ep] + peers:
        pl.semaphore_signal(barrier, inc=1, device_id=device, device_id_type=MESH)

    point = lax.broadcasted_iota(jnp.int32, (512, NB), 0)
    lane = lax.broadcasted_iota(jnp.int32, (NB, 128), 1)

    def trace_pair(k, carry):
        @pl.when(k == 0)
        def _():
            for copy in small:
                copy.wait()

        for e in (2 * k, 2 * k + 1):
            later = lax.rem(e + 2 * other, 4)
            pltpu.make_async_copy(basis.at[e], b_buf.at[e], local.at[e]).wait()
            pltpu.make_async_copy(applied.at[later], a_buf.at[later], local.at[4 + later]).start()
        traces(2 * k)
        traces(2 * k + 1)
        return carry

    def traces(e):
        turned = b_buf[e].T
        high, low = split(turned)
        picks = jnp.concatenate([face_index[e, r : r + 1, :] for r in (0, 2, 1, 3)], axis=1)
        chosen = jnp.where(point == picks, 1.0, 0.0).astype(BF16)
        values = nn(high, chosen) + nn(low, chosen)
        faces, inside = values[:, :128], values[:, 128:]
        ta[e] = faces
        tb[e] = inside
        tl[e] = jnp.where(lane < 64, faces, pltpu.roll(inside, 64, 1))
        high, low = split(turned * quad[pl.ds(e, 1), :])
        bq[0, e] = high
        bq[1, e] = low

    def rows(first, size):
        return pl.ds(pl.multiple_of(first, 8), size)

    def volume_pair(half, carry):
        for k in range(2):
            e = lax.rem(2 * half + k + 2 * other, 4)
            pltpu.make_async_copy(applied.at[e], a_buf.at[e], local.at[4 + e]).wait()
        volumes(half, 0)
        volumes(half, 1)

        @pl.when((half == 0) & (depth > 0))
        def _():
            remote("pair", 0, vpart.at[0], vpair, partner).start()

        return carry

    def volumes(half, k):
        e = lax.rem(2 * half + k + 2 * other, 4)
        first = k * 192
        faces = ta[e]
        total = three(nn, (bq[0, e], bq[1, e]), split(a_buf[e]))
        total = total + three(nt, split((2.0 * faces + tb[e]) * (1.0 / 1024.0)), split(faces))
        vpart[half, rows(first, 128), :128] = total[:128, :128]
        vpart[half, rows(first, 128), 128:] = total[:128, 128:] + total[128:, :128].T
        vpart[half, rows(first + 128, 64), :128] = total[128:192, 128:]
        vpart[half, rows(first + 128, 64), 128:] = total[192:, 128:]

    row = lax.broadcasted_iota(jnp.int32, (128, NB), 0)
    column = lax.broadcasted_iota(jnp.int32, (128, NB), 1)
    factor = jnp.where(
        column < 128,
        jnp.where(column < 64, 0.0, jnp.where(row < 64, -3.0, 0.5)),
        jnp.where(column < 192, 0.0, jnp.where(row < 64, -0.5, 0.0)),
    ) * (1.0 / 1024.0)
    slot = jnp.where(row < 64, row, row - 64)

    def couplings(i, carry):
        e = jnp.where((core == 1) | (i == 3), i, lax.rem(i + 2, 3))
        half = jnp.where(e // 2 == core, 1, 0)
        k = lax.rem(e, 2)

        @pl.when(i == 3)
        def _():
            arrive("lead", 0, tl.at[4])

        order = face_pairing[pl.ds(e, 1), :]
        order = jnp.concatenate([order] * 4, axis=1)
        mixing = jnp.where(slot == order, factor, 0.0).astype(BF16)
        high, low = split(jnp.concatenate([ta[e], tb[e]], axis=1))
        sides = nt(high, mixing) + nt(low, mixing)
        mine = rows(k * NB, NB)
        cpart[half, mine, :] = three(nt, split(sides), split(tl[e + 1]))

        @pl.when(half == 0)
        def _():
            remote("pair", 1 + k, cpart.at[0, mine], cpair.at[mine], partner).start()

        return carry

    sizes = (32, 32, 48)

    def chunk(unit, t, half):
        return rows(lax.rem(unit, 2) * NB + (half * 4 + t) * sizes[unit], sizes[unit])

    def sources(k):
        dx, dy = NEAR[k]
        return lax.rem(x + 4 - dx, 4), yh if dy == 0 else 1 - yh

    def arrived(unit, k):
        return v_in.at[k] if unit == 2 else c_in.at[unit, k]

    def part(unit):
        return vpart.at[1] if unit == 2 else cpart.at[1]

    def block(unit):
        return vblock if unit == 2 else cblock

    def scatter(unit):
        for k in range(7):
            push("scatter", unit * 7 + k, part(unit).at[chunk(unit, *chips[k])], arrived(unit, k), peers[k])

    def reduce(unit):
        where = chunk(unit, x, yh)
        total = part(unit)[where, :]
        for k in (6, 5, 4, 3, 2, 1, 0):
            arrive("scatter", unit * 7 + k, arrived(unit, k))
            total = total + arrived(unit, k)[...]
        block(unit)[where, :] = total

    def share(unit, slot, where, k):
        push("gather", unit * 7 + slot, block(unit).at[where], block(unit).at[where], peers[k])

    def gather(unit):
        where = chunk(unit, x, yh)
        if ORDERS[unit] == "direct":
            for k in range(7):
                share(unit, k, where, k)
            return
        for i, k in enumerate(ROW):
            share(unit, 1 + i, where, k)
        share(unit, 0, where, COLUMN)

    def forward(unit):
        if ORDERS[unit] == "yx":
            where = chunk(unit, x, 1 - yh)
            arrive("gather", unit * 7, block(unit).at[where])
            for i, k in enumerate(ROW):
                share(unit, 4 + i, where, k)
        if ORDERS[unit] == "xy":
            for i in (2, 1, 0):
                where = chunk(unit, sources(ROW[i])[0], yh)
                arrive("gather", unit * 7 + 1 + i, block(unit).at[where])
                share(unit, 4 + i, where, COLUMN)

    def gathered(unit):
        if ORDERS[unit] == "direct":
            for k in (6, 5, 4, 3, 2, 1, 0):
                arrive("gather", unit * 7 + k, block(unit).at[chunk(unit, *sources(k))])
            return
        for i, k in enumerate(ROW):
            t, _ = sources(k)
            if ORDERS[unit] == "yx":
                arrive("gather", unit * 7 + 1 + i, block(unit).at[chunk(unit, t, yh)])
            arrive("gather", unit * 7 + 4 + i, block(unit).at[chunk(unit, t, 1 - yh)])
        if ORDERS[unit] == "xy":
            arrive("gather", unit * 7, block(unit).at[chunk(unit, x, 1 - yh)])

    def couple(unit):
        where = rows(unit * NB, NB)
        arrive("pair", 1 + unit, cpair.at[where])
        cpart[1, where, :] = cpart[1, where, :] + cpair[where, :]
        scatter(unit)

    def doubled(value):
        high, low = split(value)
        return jnp.concatenate([high, low], axis=1)

    def times(matrix, pair):
        both = nn(matrix[0], pair)
        return both[:, :128] + (both[:, 128:] + nn(matrix[1], pair[:, :128]))

    def halo(name, n, j):
        if name == "up":
            return remote("up", n * 2 + j, up_out.at[n, j], up_in.at[n, j], after)
        return remote("down", n * 2 + j, field.at[n, j, pl.ds(0, 256)], down_in.at[n, j], before)

    def offer_up(n, j):
        up_out[n, j] = times(up_part, doubled(field[n, j, 256:, :]))
        halo("up", n, j).start()

    def meet():
        pl.semaphore_wait(barrier, 11)
        remote("lead", 0, tl.at[0], tl.at[4], em).start()
        remote("vin", 0, orbitals.at[other_rows], field.at[0, core], partner).start()

    depth = lax.rem(elem, 8)
    lax.fori_loop(0, 2, trace_pair, 0)
    pl.when(depth > 0)(meet)
    lax.fori_loop(0, 2, volume_pair, 0)
    @pl.when(depth == 0)
    def _():
        meet()
        remote("pair", 0, vpart.at[0], vpair, partner).start()

    arrive("pair", 0, vpair)
    vpart[1] = vpart[1] + vpair[...]
    scatter(2)
    lax.fori_loop(0, 4, couplings, 0)
    couple(0)
    couple(1)
    reduce(2)
    gather(2)
    reduce(1)
    gather(1)
    reduce(0)
    gather(0)
    forward(2)
    forward(1)
    gathered(1)
    outer = cblock[NB:, :] * (1.0 / 12.0)
    high, low = split(outer.T)
    up_part[0] = high
    up_part[1] = low
    high, low = split(outer)
    down_part[0] = high
    down_part[1] = low
    own_field.wait()
    arrive("vin", 0, field.at[0, other])
    for j in range(2):
        halo("down", 0, j).start()
        offer_up(0, j)
    forward(0)

    diagonal = jnp.where(
        lax.broadcasted_iota(jnp.int32, (128, 128), 0) == lax.broadcasted_iota(jnp.int32, (128, 128), 1), 4.0 / 12.0, 0.0
    )
    def halved(corner):
        return (corner + corner.T) * (0.5 / 12.0) - diagonal

    def near_store(first, second, value):
        high, low = split(value)
        near_part[0, first : first + value.shape[0], second : second + value.shape[1]] = high
        near_part[1, first : first + value.shape[0], second : second + value.shape[1]] = low

    gathered(2)
    for k in range(2):
        first = k * 192
        corner = k * NB
        near_store(corner, corner, halved(vblock[first : first + 128, :128]))
        cross = vblock[first : first + 128, 128:] * (0.5 / 12.0)
        near_store(corner, corner + 128, cross)
        near_store(corner + 128, corner, cross.T)
        last = jnp.concatenate([vblock[first + 128 : first + 192, :128], vblock[first + 128 : first + 192, 128:]], axis=0)
        near_store(corner + 128, corner + 128, halved(last))
    gathered(0)
    inner = cblock[:NB, :] * (1.0 / 12.0)
    near_store(0, NB, inner)
    near_store(NB, 0, inner.T)
    def hand_over(k):
        return remote("vout", k, field.at[4, other, pl.ds(k * NB, NB)], out.at[rows(core * 512 + k * NB, NB)], partner)

    def filter_step(m, carry):
        n = m - 1
        oldest = jnp.maximum(m - 2, 0)
        scale = jnp.where(m == 1, 1.0, 2.0)
        keep = jnp.where(m == 1, 0.0, 1.0)
        parts = [split(field[n, j]) for j in range(2)]
        high = jnp.concatenate([parts[0][0], parts[1][0]], axis=1)
        low = jnp.concatenate([parts[0][1], parts[1][1]], axis=1)
        near_sum[...] = nn(near_part[0], high) + (nn(near_part[0], low) + nn(near_part[1], high))

        def column_step(j, inner):
            lanes = pl.ds(pl.multiple_of(j * 128, 128), 128)
            halo("up", n, j).wait_recv()
            value = scale * (near_sum[:256, lanes] + up_in[n, j])
            field[m, j, :256, :] = value - keep * field[oldest, j, :256, :]

            @pl.when((m == 4) & (j == other))
            def _():
                hand_over(0).start()

            @pl.when(m < 4)
            def _():
                halo("down", m, j).start()

            halo("down", n, j).wait_recv()
            value = scale * (near_sum[256:, lanes] + times(down_part, doubled(down_in[n, j])))
            field[m, j, 256:, :] = value - keep * field[oldest, j, 256:, :]

            @pl.when(m < 4)
            def _():
                offer_up(m, j)

            @pl.when((m == 4) & (j == other))
            def _():
                hand_over(1).start()

            return inner

        return lax.fori_loop(0, 2, column_step, carry)

    lax.fori_loop(1, 5, filter_step, 0)
    out[own_rows, :] = field[4, core]

    def drain(k, carry):
        n, j = k // 2, lax.rem(k, 2)
        halo("up", n, j).wait_send()
        halo("down", n, j).wait_send()
        return carry

    lax.fori_loop(0, 8, drain, 0)
    for copy in started:
        copy.wait_send()
    sent("lead", 0, tl.at[0])
    sent("vin", 0, field.at[0, core])
    sent("pair", 0, vpart.at[0])
    for unit in range(2):
        sent("pair", 1 + unit, cpart.at[0, rows(unit * NB, NB)])
    for k in range(2):
        hand_over(k).wait_send()
        arrive("vout", k, out.at[rows(other * 512 + k * NB, NB)])


def body(basis, applied, quad, face_index, face_pairing, orbitals):
    anywhere = pl.BlockSpec(memory_space=pl.ANY)
    return pl.pallas_call(
        kernel,
        out_shape=pltpu.VMEM(orbitals.shape, F32),
        in_specs=[anywhere] * 6,
        out_specs=pl.BlockSpec(memory_space=pltpu.VMEM),
        scratch_shapes=[
            pltpu.VMEM((4, 512, NB), F32),
            pltpu.VMEM((4, 512, NB), F32),
            pltpu.VMEM(quad.shape, F32),
            pltpu.VMEM(face_index.shape, jnp.int32),
            pltpu.VMEM(face_pairing.shape, jnp.int32),
            pltpu.VMEM((2, 4, NB, 512), BF16),
            pltpu.VMEM((4, NB, 128), F32),
            pltpu.VMEM((4, NB, 128), F32),
            pltpu.VMEM((5, NB, 128), F32),
            pltpu.VMEM((2, 384, NB), F32),
            pltpu.VMEM((2, 512, NB), F32),
            pltpu.VMEM((384, NB), F32),
            pltpu.VMEM((512, NB), F32),
            pltpu.VMEM((7, 48, NB), F32),
            pltpu.VMEM((2, 7, 32, NB), F32),
            pltpu.VMEM((384, NB), F32),
            pltpu.VMEM((512, NB), F32),
            pltpu.VMEM((2, 512, 512), BF16),
            pltpu.VMEM((2, NB, NB), BF16),
            pltpu.VMEM((2, NB, NB), BF16),
            pltpu.VMEM((5, 2, 512, 128), F32),
            pltpu.VMEM((512, NB), F32),
            pltpu.VMEM((4, 2, NB, 128), F32),
            pltpu.VMEM((4, 2, NB, 128), F32),
            pltpu.VMEM((4, 2, NB, 128), F32),
            pltpu.SemaphoreType.DMA((12,)),
            pltpu.SemaphoreType.DMA((COPIES,)),
            pltpu.SemaphoreType.DMA((COPIES,)),
        ],
        name="filtered",
        compiler_params=pltpu.CompilerParams(collective_id=0, has_side_effects=True),
    )(basis, applied, quad, face_index, face_pairing, orbitals)


def solution(mesh):
    return jax.shard_map(
        body,
        mesh=mesh,
        in_specs=(
            P("elem", "pts", None),
            P("elem", "pts", None),
            P("elem", "pts"),
            P("elem", None, "pts"),
            P("elem", "pts"),
            P("elem", "pts"),
        ),
        out_specs=P("elem", "pts"),
        check_vma=False,
    )
```
